256 devices in a mesh: seq: 16 (over z, core), head: 16 (over y, x).
Axes of the slice: x: 4, y: 4, z: 8, core: 2. Of those that a mesh axis runs over, the one named last changes fastest.
Arguments:
- tokens: bfloat16 [16384, 4096], P('seq', 'head'), may hold values from -6 to 6
- w_qkv: bfloat16 [3, 4096, 4096], P(None, None, 'head'), may hold values from -0.09375 to 0.09375
- w_out: bfloat16 [4096, 4096], P('head'), may hold values from -0.125 to 0.125
- decay_rate: float32 [32, 16384], P('head', 'seq'), may hold values from 0 to 1, as said below
- prior_state: float32 [32, 128, 128], P('head'), may hold values from -384 to 384
Outputs:
- mixed: bfloat16 [16384, 4096], P('seq', 'head')
The draws below stay inside these ranges and needn't reach their ends.
Inputs may be any that keep to these rules, and one draw needn't show every extreme that they name: `decay_rate`: rates of each head for each position; every rate is positive.
All inputs are finite; a program needn't handle non-finite values.
Results may differ from the reference program's by a relative error of at most 0.02.
Values may be sent and summed in bfloat16 or wider, within the bound.
A program may use at most 64 MiB of HBM per device.

```python
import math
import jax
import jax.numpy as jnp
from jax import lax

D = 4096
DECAY_CHANNELS = 32
DH = 128
TOK_DEV = 1024
SEGMENTS = 16
HEAD_GROUPS = 16
TOKENS = 16384
N_SEQ = 16


def draw_decay_rate(key, part):
    lookup_vectors = jax.random.split(jax.random.fold_in(key, 41), 7)
    timeline_count = TOKENS
    fast_count = 5
    fast_flag = jax.random.randint(lookup_vectors[0], (DECAY_CHANNELS, 1), 0, 10) < fast_count
    fast_rate = jnp.exp(jax.random.uniform(lookup_vectors[1], (DECAY_CHANNELS, 1), jnp.float32, math.log(1.0 / 50.0), math.log(1.0 / 30.0)))
    slow_rate = jnp.exp(jax.random.uniform(lookup_vectors[2], (DECAY_CHANNELS, 1), jnp.float32, math.log(0.05), math.log(0.3))) / timeline_count
    floor_frequency = jnp.where(fast_flag, fast_rate, slow_rate)
    position = jnp.arange(timeline_count, dtype=jnp.float32)[None, :]
    phase = jax.random.uniform(lookup_vectors[3], (DECAY_CHANNELS, 1), jnp.float32, 0.0, 2.0 * math.pi)
    cyclic_waveform = jnp.exp(0.7 * jnp.sin(2.0 * math.pi * 3.0 * position / timeline_count + phase))
    stochastic_jitter = jax.random.uniform(lookup_vectors[4], (DECAY_CHANNELS, timeline_count), jnp.float32, 0.5, 1.5)
    spike_location = jax.random.randint(lookup_vectors[5], (DECAY_CHANNELS, 3), 0, timeline_count)
    spike_duration = -jnp.log(jax.random.uniform(lookup_vectors[6], (DECAY_CHANNELS, 3), jnp.float32, 0.5, 0.8))
    entry_numbers = jnp.arange(timeline_count, dtype=jnp.int32)[None, None, :]
    spike_occurrences = jnp.max(jnp.where(entry_numbers == spike_location[:, :, None], spike_duration[:, :, None], 0.0), axis=1)
    return (floor_frequency * cyclic_waveform * stochastic_jitter + spike_occurrences).astype(jnp.float32)


def with_spikes(entries, rng, source, target, parts, factor):
    owner, partner = [(jnp.arange(entries.shape[dim]) // (entries.shape[dim] // parts)).reshape([-1 if axis == dim else 1 for axis in range(entries.ndim)]) for dim in (source, target)]
    chosen = jax.random.permutation(rng, parts)[partner]
    strong = (owner == chosen) | (owner == (partner + parts // 2) % parts)
    return jnp.where(strong, factor * entries, entries)


def shard_levels(key, shape, pieces, low, top_value):
    gain, own = 1.0, jax.random.fold_in(key, 6)
    for axis_at, parts in pieces:
        heights = jnp.exp(jax.random.uniform(jax.random.fold_in(own, axis_at), (parts,), jnp.float32, low / len(pieces), top_value / len(pieces)))
        gain = gain * jnp.repeat(heights, shape[axis_at] // parts).reshape([-1 if axis == axis_at else 1 for axis in range(len(shape))])
    return gain


def bell_draw(rng, shape, spread, limit, cuts=(), kind=jnp.bfloat16):
    array = spread * jax.random.normal(rng, shape, jnp.float32)
    if cuts:
        array = array * shard_levels(rng, shape, cuts, -0.22, 0.18)
    return jnp.clip(array, -limit, limit).astype(kind)


def bell_draw_with(stream_key, shape, scale, bound, shards, heavy, kind=jnp.bfloat16):
    drawn = scale * jax.random.normal(stream_key, shape, jnp.float32)
    if shards:
        drawn = drawn * shard_levels(stream_key, shape, shards, -0.22, 0.18)
    return jnp.clip(with_spikes(drawn, jax.random.fold_in(stream_key, 3), *heavy), -bound, bound).astype(kind)


def setup_inputs(seed: int = 0) -> dict:
    streams_of = jax.random.split(jax.random.key(seed), 6)
    return {
        "tokens": bell_draw(streams_of[0], (TOKENS, D), 1.0, 6.0, ((0, 16), (1, 16))),
        "w_qkv": bell_draw(streams_of[1], (3, D, DECAY_CHANNELS * DH), D ** -0.5, 0.09375, ((2, 16),)),
        "w_out": bell_draw_with(streams_of[2], (DECAY_CHANNELS * DH, D), (DECAY_CHANNELS * DH) ** -0.5, 0.125, ((0, 16),), (0, 1, 16, 2.0)),
        "decay_rate": draw_decay_rate(jax.random.fold_in(streams_of[5], 71), 0),
        "prior_state": bell_draw(streams_of[4], (DECAY_CHANNELS, DH, DH), (0.5 * (TOK_DEV * N_SEQ) ** 0.5), 384.0, ((0, 16),), jnp.float32),
    }


def segment_terms(operands):
    queries, keys_seg, values_seg, rates = operands
    cumulative = jnp.cumsum(rates, axis=1)
    query_f = queries.astype(jnp.float32)
    key_f = keys_seg.astype(jnp.float32)
    value_f = values_seg.astype(jnp.float32)
    scores = jnp.einsum('thd,uhd->htu', query_f, key_f, precision=lax.Precision.HIGHEST)
    decay_gap = cumulative[:, :, None] - cumulative[:, None, :]
    timeline_count = rates.shape[1]
    causal = lax.broadcasted_iota(jnp.int32, (timeline_count, timeline_count), 0) >= lax.broadcasted_iota(jnp.int32, (timeline_count, timeline_count), 1)
    weights = jnp.where(causal[None], scores * jnp.exp(-jnp.maximum(decay_gap, 0.0)), 0.0)
    weights = lax.optimization_barrier(weights.astype(jnp.bfloat16)).astype(jnp.float32)
    within = jnp.einsum('htu,uhd->thd', weights, value_f, precision=lax.Precision.HIGHEST)
    tail_sum = cumulative[:, -1:]
    scaled_keys = key_f * jnp.exp(cumulative - tail_sum).T[:, :, None]
    scaled_keys = lax.optimization_barrier(scaled_keys.astype(jnp.bfloat16)).astype(jnp.float32)
    end_state = jnp.einsum('thd,the->hde', scaled_keys, value_f, precision=lax.Precision.HIGHEST)
    return (within, end_state, jnp.exp(-tail_sum[:, 0]), cumulative)

def segment_output(operands):
    queries, entering_seg, cumulative, within = operands
    rounded = lax.optimization_barrier(entering_seg.astype(jnp.bfloat16)).astype(jnp.float32)
    from_state = jnp.einsum('thd,hde->the', queries.astype(jnp.float32), rounded, precision=lax.Precision.HIGHEST)
    from_state = from_state * jnp.exp(-cumulative).T[:, :, None]
    combined = within + from_state
    normed = combined * lax.rsqrt(lax.optimization_barrier(jnp.mean(combined * combined, axis=2, keepdims=True)) + 1e-06)
    return normed.astype(jnp.bfloat16).reshape(normed.shape[0], -1)

def reference(tokens, w_qkv, w_out, decay_rate, prior_state):
    projected = [jnp.dot(tokens, w_qkv[part_index], preferred_element_type=jnp.float32).astype(jnp.bfloat16) for part_index in range(3)]
    shaped = [member.reshape(SEGMENTS, TOK_DEV, DECAY_CHANNELS, DH) for member in projected]
    rate_seg = decay_rate.reshape(DECAY_CHANNELS, SEGMENTS, TOK_DEV).transpose(1, 0, 2)
    within, end_states, end_decays, cumulative = lax.map(segment_terms, (shaped[0], shaped[1], shaped[2], rate_seg))

    def advance(state_now, pair):
        decay_seg, end_seg = pair
        return (decay_seg[:, None, None] * state_now + end_seg, state_now)
    final_state, entering = lax.scan(advance, prior_state.astype(jnp.float32), (end_decays, end_states))
    normed_all = lax.map(segment_output, (shaped[0], entering, cumulative, within)).reshape(TOKENS, DECAY_CHANNELS * DH)
    width = DECAY_CHANNELS // HEAD_GROUPS * DH

    def add_group(group, running):
        columns = lax.dynamic_slice_in_dim(normed_all, group * width, width, 1)
        rows = lax.dynamic_slice_in_dim(w_out, group * width, width, 0)
        term = jnp.dot(columns, rows, preferred_element_type=jnp.float32)
        return running + lax.optimization_barrier(term.astype(jnp.bfloat16)).astype(jnp.float32)
    summed = lax.fori_loop(0, HEAD_GROUPS, add_group, jnp.zeros((TOKENS, D), jnp.float32))
    return summed.astype(jnp.bfloat16)
```

```python
import jax
import jax.numpy as jnp
from jax import lax
from jax.experimental import pallas as pl
from jax.experimental.pallas import tpu as pltpu
from jax.sharding import PartitionSpec as P

F32 = jnp.float32
BF16 = jnp.bfloat16
TOK = 1024
HALF = 512
BLK = 256
CH = 256
NCH = TOK // CH
DH = 128
NZ = 8


def dot(a, b):
    return jnp.dot(a, b, preferred_element_type=F32)


def dot_nt(a, b):
    return lax.dot_general(a, b, (((1,), (1,)), ((), ())), preferred_element_type=F32)


def dot_tn(a, b):
    return lax.dot_general(a, b, (((0,), (0,)), ((), ())), preferred_element_type=F32)


def kernel(
    tok_hbm, wqkv_hbm, wout_hbm, rate_ref, prior_hbm, out_ref,
    X, W, WO, PRI, acc, qkv, dec, sa, sb, ce, tails, tsib, ctot,
    sloc, sown, ssib, cst, est, sful, normed, part,
    rm1, rd, qm1, qd,
    lsem, us, ur, vs, vr, ps, pr, p2s, p2r, ts, tr, cs, cr, ss, sr,
):
    seq = lax.axis_index("seq")
    head = lax.axis_index("head")
    z = seq // 2
    core = seq % 2
    y = head // 4
    x = head % 4
    first = core == 0
    u = jnp.where(first, x, y)
    v = jnp.where(first, y, x)
    su = jnp.where(first, 1, 4)
    sv = jnp.where(first, 4, 1)

    def hid(du, dv):
        return ((u + du) % 4) * su + ((v + dv) % 4) * sv

    own = hid(0, 0)
    up, um = (seq, hid(1, 0)), (seq, hid(3, 0))
    vp, vm = (seq, hid(0, 1)), (seq, hid(0, 3))
    zp = (((z + 1) % NZ) * 2 + core, head)
    zm = (((z + NZ - 1) % NZ) * 2 + core, head)
    sib = (z * 2 + 1 - core, head)

    def rdma(src, dst, s, r, dev):
        return pltpu.make_async_remote_copy(
            src_ref=src, dst_ref=dst, send_sem=s, recv_sem=r,
            device_id=dev, device_id_type=pl.DeviceIdType.MESH,
        )

    ltok = pltpu.make_async_copy(tok_hbm, X.at[own], lsem.at[0])
    lw = pltpu.make_async_copy(wqkv_hbm, W, lsem.at[1])
    lwo = pltpu.make_async_copy(wout_hbm, WO, lsem.at[2])
    lpri = pltpu.make_async_copy(prior_hbm, PRI, lsem.at[3])
    ltok.start()
    lw.start()
    lwo.start()
    lpri.start()

    barrier = pltpu.get_barrier_semaphore()
    for dev in (up, um, vp, vm, zp, zm, sib):
        pl.semaphore_signal(barrier, inc=1, device_id=dev, device_id_type=pl.DeviceIdType.MESH)
    pl.semaphore_wait(barrier, 7)
    ltok.wait()

    def xs(blk, hf):
        return X.at[blk, pl.ds(hf * HALF, HALF)]

    def ag(blk, hf, sems, k, dev):
        return rdma(xs(blk, hf), xs(blk, hf), sems[0].at[k], sems[1].at[k], dev)

    usem, vsem = (us, ur), (vs, vr)
    DU = (0, 3, 1, 2)

    def vsend(b, hf):
        blk = hid(DU[b], 0)
        if hf == 0:
            ag(blk, 0, vsem, 6 * b + 0, vp).start()
            ag(blk, 0, vsem, 6 * b + 4, vm).start()
        else:
            ag(blk, 1, vsem, 6 * b + 3, vm).start()
            ag(blk, 1, vsem, 6 * b + 1, vp).start()

    ag(own, 0, usem, 0, up).start()
    ag(own, 1, usem, 3, um).start()
    ag(own, 1, usem, 1, up).start()
    ag(own, 0, usem, 4, um).start()
    vsend(0, 0)
    vsend(0, 1)

    rowi = lax.broadcasted_iota(jnp.int32, (CH, CH), 0)
    coli = lax.broadcasted_iota(jnp.int32, (CH, CH), 1)
    for h in range(2):
        def one_decay(c, carry):
            i = h * NCH + c
            r = rate_ref[h : h + 1, pl.ds(pl.multiple_of(c * CH, CH), CH)]
            rb = jnp.broadcast_to(r, (CH, CH))
            zero = jnp.zeros((CH, CH), F32)
            c_col = jnp.sum(jnp.where(coli <= rowi, rb, zero), axis=1, keepdims=True)
            r_col = jnp.sum(jnp.where(coli == rowi, rb, zero), axis=1, keepdims=True)
            c_row = jnp.sum(
                jnp.where(rowi <= coli, jnp.broadcast_to(r_col, (CH, CH)), zero),
                axis=0, keepdims=True,
            )
            total = jnp.sum(r, axis=1, keepdims=True)
            gap = jnp.maximum(c_col - c_row, 0.0)
            dec[i] = jnp.where(rowi >= coli, jnp.exp(-gap), zero)
            sa[i] = jnp.broadcast_to(jnp.exp(-c_col), (CH, DH))
            sb[i] = jnp.broadcast_to(jnp.exp(-jnp.maximum(total - c_col, 0.0)), (CH, DH))
            ce[i] = jnp.broadcast_to(total, (8, DH))
            return carry

        lax.fori_loop(0, NCH, one_decay, 0)
        tails[h] = ce[h * NCH] + ce[h * NCH + 1] + ce[h * NCH + 2] + ce[h * NCH + 3]

    tsend = rdma(tails, tsib, ss.at[0], sr.at[0], sib)
    tsend.start()

    def zero_acc(i, carry):
        acc[i // 4, pl.ds((i % 4) * CH, CH)] = jnp.zeros((CH, BLK), F32)
        return carry

    lax.fori_loop(0, 12, zero_acc, 0)

    ag(hid(3, 0), 0, usem, 0, up).wait_recv()
    ag(hid(3, 0), 0, usem, 2, up).start()
    ag(hid(1, 0), 1, usem, 3, um).wait_recv()
    ag(hid(1, 0), 1, usem, 5, um).start()
    vsend(1, 0)
    vsend(2, 1)
    ag(hid(3, 0), 1, usem, 1, up).wait_recv()
    vsend(1, 1)
    ag(hid(1, 0), 0, usem, 4, um).wait_recv()
    vsend(2, 0)
    ag(hid(2, 0), 0, usem, 2, up).wait_recv()
    vsend(3, 0)
    ag(hid(2, 0), 1, usem, 5, um).wait_recv()
    vsend(3, 1)

    lw.wait()

    def mm(blk):
        off = pl.multiple_of(blk * BLK, BLK)

        def rows_mm(r, carry):
            rows = pl.ds(pl.multiple_of(r * CH, CH), CH)
            xt = X[blk, rows, :]
            for c in range(3):
                acc[c, rows, :] += dot(xt, W[c, pl.ds(off, BLK), :])
            return carry

        lax.fori_loop(0, NCH, rows_mm, 0)

    tsend.wait_recv()
    ctot[z] = tails[...] + tsib[...]

    def ring(buf, sems, d, k, slot, dev):
        return rdma(buf.at[slot], buf.at[slot], sems[0].at[d * 4 + k], sems[1].at[d * 4 + k], dev)

    def ring_start(buf, sems):
        ring(buf, sems, 0, 0, z, zp).start()
        ring(buf, sems, 1, 0, z, zm).start()

    def ring_step(buf, sems, k):
        a = (z + NZ - k) % NZ
        ring(buf, sems, 0, k - 1, a, zp).wait_recv()
        if k < 4:
            ring(buf, sems, 0, k, a, zp).start()
            b = (z + k) % NZ
            ring(buf, sems, 1, k - 1, b, zm).wait_recv()
            if k < 3:
                ring(buf, sems, 1, k, b, zm).start()

    tsem, csem = (ts, tr), (cs, cr)
    ring_start(ctot, tsem)

    for b in range(4):
        ag(hid(DU[b], 3), 0, vsem, 6 * b + 0, vp).wait_recv()
        ag(hid(DU[b], 3), 0, vsem, 6 * b + 2, vp).start()
        ag(hid(DU[b], 1), 1, vsem, 6 * b + 3, vm).wait_recv()
        ag(hid(DU[b], 1), 1, vsem, 6 * b + 5, vm).start()
        mm(hid(DU[b], 0))
        ring_step(ctot, tsem, b + 1)

    def du_of(b):
        return jnp.where(b == 1, 3, jnp.where(b == 2, 1, jnp.where(b == 3, 2, 0)))

    def gather_rest(b, carry):
        du = du_of(b)
        ag(hid(du, 3), 1, vsem, 6 * b + 1, vp).wait_recv()
        mm(hid(du, 3))
        ag(hid(du, 1), 0, vsem, 6 * b + 4, vm).wait_recv()
        mm(hid(du, 1))
        ag(hid(du, 2), 0, vsem, 6 * b + 2, vp).wait_recv()
        ag(hid(du, 2), 1, vsem, 6 * b + 5, vm).wait_recv()
        mm(hid(du, 2))
        return carry

    lax.fori_loop(0, 4, gather_rest, 0)

    def to_bf16(i, carry):
        rows = pl.ds(pl.multiple_of((i % 4) * CH, CH), CH)
        qkv[i // 4, rows, :] = acc[i // 4, rows, :].astype(BF16)
        return carry

    lax.fori_loop(4, 12, to_bf16, 0)
    for h in range(2):
        lanes = slice(h * DH, (h + 1) * DH)
        state = jnp.zeros((DH, DH), F32)
        for c in range(NCH):
            i = h * NCH + c
            rows = slice(c * CH, (c + 1) * CH)
            ks = (qkv[1, rows, lanes].astype(F32) * sb[i]).astype(BF16)
            kv = dot_tn(ks, qkv[2, rows, lanes])
            sloc[i] = state
            state = jnp.exp(-ce[i, 0:1, :]) * state + kv
        sown[h] = state
    ssend = rdma(sown, ssib, ss.at[1], sr.at[1], sib)
    ssend.start()
    lax.fori_loop(0, 4, to_bf16, 0)

    def intra(c):
        rows = slice(c * CH, (c + 1) * CH)
        for h in range(2):
            lanes = slice(h * DH, (h + 1) * DH)
            s = dot_nt(qkv[0, rows, lanes], qkv[1, rows, lanes])
            w = (s * dec[h * NCH + c]).astype(BF16)
            acc[0, rows, lanes] = dot(w, qkv[2, rows, lanes])

    ssend.wait_recv()
    mine, other = sown[core], ssib[core]
    t_own, t_sib = tails[core, 0:1, :], tsib[core, 0:1, :]
    s_even = jnp.where(first, mine, other)
    s_odd = jnp.where(first, other, mine)
    t_odd = jnp.where(first, t_sib, t_own)
    cst[z] = (jnp.exp(-t_odd) * s_even + s_odd).astype(BF16)
    ring_start(cst, csem)
    for k in range(4):
        intra(k)
        ring_step(cst, csem, k + 1)

    lpri.wait()
    run = jnp.zeros((1, DH), F32)
    ent = jnp.zeros((DH, DH), F32)
    for i in range(NZ - 1, -1, -1):
        earlier = i < z
        ent = ent + jnp.where(earlier, jnp.exp(-run) * cst[i].astype(F32), 0.0)
        run = run + jnp.where(earlier, ctot[i, core, 0:1, :], 0.0)
    est[core] = ent + jnp.exp(-run) * PRI[core]
    esend = rdma(est.at[core], est.at[core], ss.at[2], sr.at[2], sib)
    esend.start()
    rdma(est.at[1 - core], est.at[1 - core], ss.at[2], sr.at[2], sib).wait_recv()

    for h in range(2):
        lanes = slice(h * DH, (h + 1) * DH)
        e = est[h]
        e = jnp.where(first, e, jnp.exp(-tsib[h, 0:1, :]) * e + ssib[h])
        before = jnp.zeros((1, DH), F32)
        for c in range(NCH):
            i = h * NCH + c
            sful[i] = (sloc[i] + jnp.exp(-before) * e).astype(BF16)
            before = before + ce[i, 0:1, :]
        for c in range(NCH):
            i = h * NCH + c
            rows = slice(c * CH, (c + 1) * CH)
            f = dot(qkv[0, rows, lanes], sful[i])
            comb = acc[0, rows, lanes] + f * sa[i]
            ms = jnp.mean(comb * comb, axis=1, keepdims=True)
            normed[rows, lanes] = (comb * lax.rsqrt(ms + 1e-06)).astype(BF16)

    lwo.wait()
    RU = (2, 1, 3, 0)

    def ru_of(i):
        return jnp.where(i == 0, 2, jnp.where(i == 1, 1, jnp.where(i == 2, 3, 0)))

    def proj(blk):
        off = pl.multiple_of(blk * BLK, BLK)

        def rows_pj(r, carry):
            rows = pl.ds(pl.multiple_of(r * CH, CH), CH)
            part[blk, rows, :] = dot(normed[rows, :], WO[:, pl.ds(off, BLK)]).astype(BF16)
            return carry

        lax.fori_loop(0, NCH, rows_pj, 0)

    def ph(blk, hf):
        return part.at[blk, pl.ds(hf * HALF, HALF)]

    def m1(i, d):
        return rdma(
            ph(hid(ru_of(i), 2), d), rm1.at[d, i], ps.at[6 * i + 3 * d], pr.at[6 * i + 3 * d],
            vp if d == 0 else vm,
        )

    def m2(i, d):
        return rdma(
            ph(hid(ru_of(i), 1 if d == 0 else 3), 1 - d), rd.at[d, i, pl.ds((1 - d) * HALF, HALF)],
            ps.at[6 * i + 3 * d + 1], pr.at[6 * i + 3 * d + 1], vp if d == 0 else vm,
        )

    def m3(i, d):
        return rdma(
            ph(hid(ru_of(i), 1 if d == 0 else 3), d), rd.at[d, i, pl.ds(d * HALF, HALF)],
            ps.at[6 * i + 3 * d + 2], pr.at[6 * i + 3 * d + 2], vp if d == 0 else vm,
        )

    def add_half(blk, hf, ref):
        for r in range(2):
            rows = pl.ds(hf * HALF + r * CH, CH)
            part[blk, rows, :] = (
                part[blk, rows, :].astype(F32) + ref[pl.ds(r * CH, CH), :].astype(F32)
            ).astype(BF16)

    def rs1(i, carry):
        proj(hid(ru_of(i), 2))
        m1(i, 0).start()
        m1(i, 1).start()
        return carry

    def rs2(i, carry):
        for d in range(2):
            proj(hid(ru_of(i), 1 if d == 0 else 3))
            m2(i, d).start()
        return carry

    def rs3(i, carry):
        for d in range(2):
            m1(i, d).wait_recv()
            add_half(hid(ru_of(i), 1 if d == 0 else 3), d, rm1.at[d, i])
            m3(i, d).start()
        proj(hid(ru_of(i), 0))
        return carry

    lax.fori_loop(0, 4, rs1, 0)
    lax.fori_loop(0, 4, rs2, 0)
    lax.fori_loop(0, 4, rs3, 0)

    def q1(d):
        return rdma(ph(hid(2, 0), d), qm1.at[d], p2s.at[3 * d], p2r.at[3 * d], up if d == 0 else um)

    def q2(d):
        return rdma(
            ph(hid(1 if d == 0 else 3, 0), 1 - d), qd.at[d, pl.ds((1 - d) * HALF, HALF)],
            p2s.at[3 * d + 1], p2r.at[3 * d + 1], up if d == 0 else um,
        )

    def q3(d):
        return rdma(
            ph(hid(1 if d == 0 else 3, 0), d), qd.at[d, pl.ds(d * HALF, HALF)],
            p2s.at[3 * d + 2], p2r.at[3 * d + 2], up if d == 0 else um,
        )

    for i in range(4):
        blk = hid(RU[i], 0)
        for d in range(2):
            m2(i, d).wait_recv()
            m3(i, d).wait_recv()

        def reduce_rows(r, carry):
            rows = pl.ds(pl.multiple_of(r * CH, CH), CH)
            part[blk, rows, :] = (
                part[blk, rows, :].astype(F32)
                + rd[0, i, rows, :].astype(F32)
                + rd[1, i, rows, :].astype(F32)
            ).astype(BF16)
            return carry

        lax.fori_loop(0, NCH, reduce_rows, 0)
        if i == 0:
            q1(0).start()
            q1(1).start()
        elif i == 1:
            q2(0).start()
        elif i == 2:
            q2(1).start()
    for d in range(2):
        q1(d).wait_recv()
        add_half(hid(1 if d == 0 else 3, 0), d, qm1.at[d])
        q3(d).start()
    for d in range(2):
        q2(d).wait_recv()
    for d in range(2):
        q3(d).wait_recv()

    def finish(r, carry):
        rows = pl.ds(pl.multiple_of(r * CH, CH), CH)
        out_ref[rows, :] = (
            part[own, rows, :].astype(F32) + qd[0, rows, :].astype(F32) + qd[1, rows, :].astype(F32)
        ).astype(BF16)
        return carry

    lax.fori_loop(0, NCH, finish, 0)

    for k in range(6):
        ag(own, 0, usem, k, up).wait_send()

    def drain_ag(k, carry):
        ag(own, 0, vsem, k, vp).wait_send()
        return carry

    lax.fori_loop(0, 24, drain_ag, 0)
    for buf, sems in ((ctot, tsem), (cst, csem)):
        for k in range(4):
            ring(buf, sems, 0, k, z, zp).wait_send()
        for k in range(3):
            ring(buf, sems, 1, k, z, zm).wait_send()
    tsend.wait_send()
    ssend.wait_send()
    esend.wait_send()

    def drain_rs(i, carry):
        for d in range(2):
            m1(i, d).wait_send()
            m2(i, d).wait_send()
            m3(i, d).wait_send()
        return carry

    lax.fori_loop(0, 4, drain_rs, 0)
    for d in range(2):
        q1(d).wait_send()
        q2(d).wait_send()
        q3(d).wait_send()


def local(tokens, w_qkv, w_out, decay_rate, prior_state):
    anyspec = pl.BlockSpec(memory_space=pl.ANY)
    vspec = pl.BlockSpec(memory_space=pltpu.VMEM)
    V = pltpu.VMEM
    D = pltpu.SemaphoreType.DMA
    return pl.pallas_call(
        kernel,
        out_shape=jax.ShapeDtypeStruct((TOK, BLK), BF16),
        in_specs=[anyspec, anyspec, anyspec, vspec, anyspec],
        out_specs=vspec,
        scratch_shapes=[
            V((16, TOK, BLK), BF16),
            V((3, 4096, BLK), BF16),
            V((BLK, 4096), BF16),
            V((2, DH, DH), F32),
            V((3, TOK, BLK), F32),
            V((3, TOK, BLK), BF16),
            V((8, CH, CH), F32),
            V((8, CH, DH), F32),
            V((8, CH, DH), F32),
            V((8, 8, DH), F32),
            V((2, 8, DH), F32),
            V((2, 8, DH), F32),
            V((NZ, 2, 8, DH), F32),
            V((8, DH, DH), F32),
            V((2, DH, DH), F32),
            V((2, DH, DH), F32),
            V((NZ, DH, DH), BF16),
            V((2, DH, DH), F32),
            V((8, DH, DH), BF16),
            V((TOK, BLK), BF16),
            V((16, TOK, BLK), BF16),
            V((2, 4, HALF, BLK), BF16),
            V((2, 4, TOK, BLK), BF16),
            V((2, HALF, BLK), BF16),
            V((2, TOK, BLK), BF16),
            D((4,)),
            D((6,)), D((6,)),
            D((24,)), D((24,)),
            D((24,)), D((24,)),
            D((6,)), D((6,)),
            D((8,)), D((8,)),
            D((8,)), D((8,)),
            D((3,)), D((3,)),
        ],
        compiler_params=pltpu.CompilerParams(
            collective_id=0, has_side_effects=True, vmem_limit_bytes=60 * 1024 * 1024
        ),
    )(tokens, w_qkv, w_out, decay_rate, prior_state)


def solution(mesh):
    in_specs = (
        P("seq", "head"),
        P(None, None, "head"),
        P("head", None),
        P("head", "seq"),
        P("head", None, None),
    )
    out_specs = P("seq", "head")
    return jax.shard_map(local, mesh=mesh, in_specs=in_specs, out_specs=out_specs, check_vma=False)
```

```python
import jax
import jax.numpy as jnp
from jax import lax
from jax.experimental import pallas as pl
from jax.experimental.pallas import tpu as pltpu
from jax.sharding import PartitionSpec as P

F32 = jnp.float32
BF16 = jnp.bfloat16
TOK = 1024
HALF = 512
QTR = 256
BLK = 256
CH = 256
NCH = TOK // CH
DH = 128
NZ = 8


def dot(a, b):
    return jnp.dot(a, b, preferred_element_type=F32)


def dot_nt(a, b):
    return lax.dot_general(a, b, (((1,), (1,)), ((), ())), preferred_element_type=F32)


def dot_tn(a, b):
    return lax.dot_general(a, b, (((0,), (0,)), ((), ())), preferred_element_type=F32)


def kernel(
    tok_hbm, wqkv_hbm, wout_hbm, rate_ref, prior_hbm, out_ref,
    X, tokv, W, WO, PRI, rate, acc, intra_o, qkv, dec, sa, sb, ce, tails, tpar, ctot,
    sloc, sown, spar, cst, est, sful, normed, part, sibr, pxr, m1r, rd, xbr, fin,
    lsem, es, er, ys, yr, xs, xr, fs, fr, ws, wr, qs, qr, wos, wor, ms, mr,
    ts, tr, cs, cr, sbs, sbr, pxs, pxq, m1s, m1q, m2s, m2q, m3s, m3q, xbs, xbq, fns, fnr,
):
    seq = lax.axis_index("seq")
    head = lax.axis_index("head")
    z = seq // 2
    c = seq % 2
    y = head // 4
    x = head % 4
    p = x // 2
    first = p == 0
    native = c == p
    foreign = c != p
    xp = 3 - x
    xn = x + 1 - 2 * (x % 2)
    xq = 3 - xn
    cols = (x, xn, xp, xq)

    def B(b, dy):
        return ((y + dy) % 4) * 4 + cols[b]

    def at(cc, xx):
        return (z * 2 + cc, y * 4 + xx)

    sib = at(1 - c, x)
    par = at(c, xp)
    diag = at(1 - c, xp)
    pn = at(c, xn)
    yp = (seq, ((y + 1) % 4) * 4 + x)
    ym = (seq, ((y + 3) % 4) * 4 + x)
    zp = (((z + 1) % NZ) * 2 + c, head)
    zm = (((z + NZ - 1) % NZ) * 2 + c, head)

    def rdma(src, dst, s, r, dev):
        return pltpu.make_async_remote_copy(
            src_ref=src, dst_ref=dst, send_sem=s, recv_sem=r,
            device_id=dev, device_id_type=pl.DeviceIdType.MESH,
        )

    own = B(0, 0)
    ltok = pltpu.make_async_copy(tok_hbm, tokv, lsem.at[0])
    lown = pltpu.make_async_copy(tok_hbm, X.at[own], lsem.at[1])
    lkv = pltpu.make_async_copy(wqkv_hbm.at[pl.ds(1, 2)], W.at[pl.ds(1, 2)], lsem.at[2])
    lq = pltpu.make_async_copy(wqkv_hbm.at[0], W.at[0], lsem.at[3])
    lwo = pltpu.make_async_copy(wout_hbm, WO, lsem.at[4])
    lpri = pltpu.make_async_copy(prior_hbm, PRI, lsem.at[5])
    ltok.start()

    @pl.when(native)
    def _():
        lown.start()
        lkv.start()
        lq.start()
        lwo.start()
        lpri.start()

    barrier = pltpu.get_barrier_semaphore()
    for dev in (sib, at(0, xn), at(1, xn), at(0, xp), at(1, xp), yp, ym, zp, zm):
        pl.semaphore_signal(barrier, inc=1, device_id=dev, device_id_type=pl.DeviceIdType.MESH)
    pl.semaphore_wait(barrier, 9)
    ltok.wait()

    def hf(blk, half):
        return X.at[blk, pl.ds(half * HALF, HALF)]

    tx = jnp.where(native, xn, xp)
    e_sem = er.at[jnp.where(native, 0, 1)]

    def esend(cc):
        return rdma(tokv.at[pl.ds(cc * HALF, HALF)], hf(own, cc), es.at[cc], e_sem, at(cc, tx))

    def erecv(k, b):
        return rdma(hf(B(b, 0), c), hf(B(b, 0), c), es.at[2], er.at[k], pn)

    esend(0).start()
    esend(1).start()
    e0 = rdma(tokv, X.at[own], es.at[3], er.at[3], sib)

    def kv(m, d, share, idx, dev):
        w = W.at[1 + m, pl.ds(share * 512 + d * 256, 256)]
        return rdma(w, w, ws.at[d * 16 + idx * 2 + m], wr.at[d * 16 + idx * 2 + m], dev)

    def qmsg(k):
        w = W.at[0, pl.ds(k * 1024, 1024)]
        return rdma(w, w, qs.at[k], qr.at[k], par)

    pri_send = rdma(PRI, PRI, ms.at[0], mr.at[0], par)
    rate_send = rdma(rate_ref, rate, ms.at[1], mr.at[1], diag)

    ORDER = (
        (1, 2), (3, 2), (0, 2), (2, 2),
        (1, 1), (1, 3), (3, 1), (3, 3), (0, 1), (0, 3), (2, 1), (2, 3),
        (3, 0), (1, 0), (2, 0), (0, 0),
    )
    pcols = (xp, xq, x, xn)

    def wo_msg(o, blk):
        w = WO.at[:, pl.ds(pl.multiple_of(blk * BLK, BLK), BLK)]
        return rdma(w, w, wos.at[o], wor.at[o], par)

    def wo_send(lo, hi):
        for o in range(lo, hi):
            b, dy = ORDER[o]
            wo_msg(o, ((y + dy) % 4) * 4 + pcols[b]).start()

    @pl.when(native)
    def _():
        e0.start()
        lkv.wait()
        for m in range(2):
            for d in range(2):
                kv(m, d, z, 0, par).start()
        lq.wait()
        for k in range(4):
            qmsg(k).start()
        lpri.wait()
        pri_send.start()
        lwo.wait()
        wo_send(0, 3)
        lown.wait()
        rate[...] = rate_ref[...]

    @pl.when(foreign)
    def _():
        rate_send.start()
        e0.wait_recv()

    def q_(blk, s):
        return X.at[blk, pl.ds(c * HALF + s * QTR, QTR)]

    def ym_q(b, dy, s, k, dev):
        return rdma(q_(B(b, dy), s), q_(B(b, dy), s), ys.at[6 * b + k], yr.at[6 * b + k], dev)

    def ym_h(b, dy, k, dev):
        return rdma(hf(B(b, dy), c), hf(B(b, dy), c), ys.at[6 * b + k], yr.at[6 * b + k], dev)

    def ysend(b):
        if b % 2 == 0:
            ym_q(b, 0, 0, 0, yp).start()
            ym_q(b, 0, 1, 3, ym).start()
            ym_q(b, 0, 1, 1, yp).start()
            ym_q(b, 0, 0, 4, ym).start()
        else:
            ym_h(b, 0, 0, yp).start()
            ym_h(b, 0, 3, ym).start()

    def yrelay(b):
        ym_q(b, 3, 0, 0, yp).wait_recv()
        ym_q(b, 3, 0, 2, yp).start()
        ym_q(b, 1, 1, 3, ym).wait_recv()
        ym_q(b, 1, 1, 5, ym).start()

    def sf(b, dy):
        i = b * 4 + dy
        return rdma(hf(B(b, dy), c), hf(B(b, dy), c), fs.at[i], fr.at[i], sib)

    def pxsend(j):
        return rdma(hf(B(2 * j, 2), c), hf(B(2 * j, 2), c), xs.at[j], xr.at[j], pn)

    def ring_w(k):
        @pl.when(foreign)
        def _():
            for m in range(2):
                for d in range(2):
                    share = (z + (NZ - k if d == 0 else k)) % NZ
                    kv(m, d, share, k, zp).wait_recv()
                    if k < 7:
                        kv(m, d, share, k + 1, zp if d == 0 else zm).start()

    def ring(buf, sems, d, k, slot, dev):
        return rdma(buf.at[slot], buf.at[slot], sems[0].at[d * 4 + k], sems[1].at[d * 4 + k], dev)

    def ring_start(buf, sems):
        ring(buf, sems, 0, 0, z, zp).start()
        ring(buf, sems, 1, 0, z, zm).start()

    def ring_step(buf, sems, k):
        a = (z + NZ - k) % NZ
        ring(buf, sems, 0, k - 1, a, zp).wait_recv()
        if k < 4:
            ring(buf, sems, 0, k, a, zp).start()
            b = (z + k) % NZ
            ring(buf, sems, 1, k - 1, b, zm).wait_recv()
            if k < 3:
                ring(buf, sems, 1, k, b, zm).start()

    tsem, csem = (ts, tr), (cs, cr)
    tsend = rdma(tails, tpar, ms.at[2], mr.at[2], par)

    rowi = lax.broadcasted_iota(jnp.int32, (CH, CH), 0)
    coli = lax.broadcasted_iota(jnp.int32, (CH, CH), 1)

    def decay(i):
        h, ch = i // NCH, i % NCH
        r = rate[h : h + 1, ch * CH : (ch + 1) * CH]
        rb = jnp.broadcast_to(r, (CH, CH))
        zero = jnp.zeros((CH, CH), F32)
        c_col = jnp.sum(jnp.where(coli <= rowi, rb, zero), axis=1, keepdims=True)
        r_col = jnp.sum(jnp.where(coli == rowi, rb, zero), axis=1, keepdims=True)
        c_row = jnp.sum(
            jnp.where(rowi <= coli, jnp.broadcast_to(r_col, (CH, CH)), zero),
            axis=0, keepdims=True,
        )
        total = jnp.sum(r, axis=1, keepdims=True)
        gap = jnp.maximum(c_col - c_row, 0.0)
        dec[i] = jnp.where(rowi >= coli, jnp.exp(-gap), zero)
        sa[i] = jnp.broadcast_to(jnp.exp(-c_col), (CH, DH))
        sb[i] = jnp.broadcast_to(jnp.exp(-jnp.maximum(total - c_col, 0.0)), (CH, DH))
        ce[i] = jnp.broadcast_to(total, (8, DH))

    ysend(0)
    yrelay(0)
    erecv(1, 2).wait_recv()
    e3 = rdma(hf(B(2, 0), c), hf(B(2, 0), c), es.at[2], er.at[2], pn)
    e3.start()
    ysend(2)
    sf(2, 0).start()
    erecv(0, 1).wait_recv()
    ysend(1)
    sf(1, 0).start()
    ring_w(0)

    @pl.when(foreign)
    def _():
        rdma(rate_ref, rate, ms.at[1], mr.at[1], diag).wait_recv()

    for h in range(2):
        tails[h] = jnp.broadcast_to(jnp.sum(rate[h : h + 1, :], axis=1, keepdims=True), (8, DH))
    tsend.start()
    yrelay(2)
    erecv(2, 3).wait_recv()
    ysend(3)
    sf(3, 0).start()
    ring_w(1)
    decay(0)
    tsend.wait_recv()
    ctot[z] = tails[...] + tpar[...]
    ring_start(ctot, tsem)

    def y_rest(b):
        if b % 2 == 0:
            ym_q(b, 3, 1, 1, yp).wait_recv()
            sf(b, 3).start()
            ym_q(b, 1, 0, 4, ym).wait_recv()
            sf(b, 1).start()
        else:
            ym_h(b, 3, 0, yp).wait_recv()
            sf(b, 3).start()
            ym_h(b, 1, 3, ym).wait_recv()
            sf(b, 1).start()

    def y_far(b):
        ym_q(b, 2, 0, 2, yp).wait_recv()
        ym_q(b, 2, 1, 5, ym).wait_recv()
        sf(b, 2).start()
        pxsend(b // 2).start()

    y_rest(0)
    ring_w(2)
    decay(1)
    ring_step(ctot, tsem, 1)
    y_rest(2)
    ring_w(3)
    decay(2)
    ring_step(ctot, tsem, 2)
    y_far(0)
    y_rest(1)
    ring_w(4)
    decay(3)
    ring_step(ctot, tsem, 3)
    y_far(2)
    ring_w(5)
    decay(4)
    ring_step(ctot, tsem, 4)
    decay(5)
    y_rest(3)
    ring_w(6)
    decay(6)
    for j in range(2):
        b = 1 + 2 * j
        rdma(hf(B(b, 2), c), hf(B(b, 2), c), xs.at[j], xr.at[j], pn).wait_recv()
        sf(b, 2).start()
    ring_w(7)
    decay(7)

    def mm_kv(dys, last):
        blks = [B(b, dy) for dy in dys for b in range(4)]

        def rows_mm(r, carry):
            rows = pl.ds(pl.multiple_of(r * CH, CH), CH)
            for m in range(2):
                s = acc[m, rows, :] if last else None
                for blk in blks:
                    off = pl.multiple_of(blk * BLK, BLK)
                    d = dot(X[blk, rows, :], W[1 + m, pl.ds(off, BLK), :])
                    s = d if s is None else s + d
                if last:
                    qkv[1 + m, rows, :] = s.astype(BF16)
                else:
                    acc[m, rows, :] = s
            return carry

        lax.fori_loop(0, NCH, rows_mm, 0)

    def sf_recv(dy):
        for b in range(4):
            if (b, dy) != (0, 0):
                sf(b, dy).wait_recv()

    for dy in (0, 1, 3):
        sf_recv(dy)
    mm_kv((0, 1, 3), False)
    sf_recv(2)
    mm_kv((2,), True)

    for h in range(2):
        lanes = slice(h * DH, (h + 1) * DH)
        state = jnp.zeros((DH, DH), F32)
        for ch in range(NCH):
            i = h * NCH + ch
            rows = slice(ch * CH, (ch + 1) * CH)
            ks = (qkv[1, rows, lanes].astype(F32) * sb[i]).astype(BF16)
            kvp = dot_tn(ks, qkv[2, rows, lanes])
            sloc[i] = state
            state = jnp.exp(-ce[i, 0:1, :]) * state + kvp
        sown[h] = state
    ssend = rdma(sown, spar, ms.at[3], mr.at[3], par)
    ssend.start()

    @pl.when(native)
    def _():
        wo_send(3, 9)

    @pl.when(foreign)
    def _():
        for k in range(4):
            qmsg(k).wait_recv()

    def mm_q(ch):
        rows = slice(ch * CH, (ch + 1) * CH)
        s = None
        for blk in range(16):
            d = dot(X[blk, rows, :], W[0, blk * BLK : (blk + 1) * BLK, :])
            s = d if s is None else s + d
        qkv[0, rows, :] = s.astype(BF16)

    def intra(ch):
        rows = slice(ch * CH, (ch + 1) * CH)
        for h in range(2):
            lanes = slice(h * DH, (h + 1) * DH)
            s = dot_nt(qkv[0, rows, lanes], qkv[1, rows, lanes])
            w = (s * dec[h * NCH + ch]).astype(BF16)
            intra_o[rows, lanes] = dot(w, qkv[2, rows, lanes])

    ssend.wait_recv()
    mine, other = sown[p], spar[p]
    t_own, t_par = tails[p, 0:1, :], tpar[p, 0:1, :]
    s_even = jnp.where(first, mine, other)
    s_odd = jnp.where(first, other, mine)
    t_odd = jnp.where(first, t_par, t_own)
    cst[z] = (jnp.exp(-t_odd) * s_even + s_odd).astype(BF16)
    ring_start(cst, csem)
    for k in range(4):
        mm_q(k)
        intra(k)
        ring_step(cst, csem, k + 1)

    @pl.when(foreign)
    def _():
        pri_send.wait_recv()

    run = jnp.zeros((1, DH), F32)
    ent = jnp.zeros((DH, DH), F32)
    for i in range(NZ - 1, -1, -1):
        earlier = i < z
        ent = ent + jnp.where(earlier, jnp.exp(-run) * cst[i].astype(F32), 0.0)
        run = run + jnp.where(earlier, ctot[i, p, 0:1, :], 0.0)
    est[p] = ent + jnp.exp(-run) * PRI[p]
    ent_send = rdma(est.at[p], est.at[p], ms.at[4], mr.at[4], par)
    ent_send.start()

    @pl.when(native)
    def _():
        wo_send(9, 16)

    rdma(est.at[1 - p], est.at[1 - p], ms.at[4], mr.at[4], par).wait_recv()

    for h in range(2):
        lanes = slice(h * DH, (h + 1) * DH)
        e = est[h]
        e = jnp.where(first, e, jnp.exp(-tpar[h, 0:1, :]) * e + spar[h])
        before = jnp.zeros((1, DH), F32)
        for ch in range(NCH):
            i = h * NCH + ch
            sful[i] = (sloc[i] + jnp.exp(-before) * e).astype(BF16)
            before = before + ce[i, 0:1, :]
        for ch in range(NCH):
            i = h * NCH + ch
            rows = slice(ch * CH, (ch + 1) * CH)
            f = dot(qkv[0, rows, lanes], sful[i])
            comb = intra_o[rows, lanes] + f * sa[i]
            mean = jnp.mean(comb * comb, axis=1, keepdims=True)
            normed[rows, lanes] = (comb * lax.rsqrt(mean + 1e-06)).astype(BF16)

    def ph(blk, half):
        return part.at[blk, pl.ds(half * HALF, HALF)]

    def pq(blk, s):
        return part.at[blk, pl.ds(c * HALF + s * QTR, QTR)]

    def sb_msg(o):
        return rdma(ph(B(*ORDER[o]), 1 - c), sibr.at[o], sbs.at[o], sbr.at[o], sib)

    def proj(o):
        blk = B(*ORDER[o])

        @pl.when(foreign)
        def _():
            wo_msg(o, blk).wait_recv()

        off = pl.multiple_of(blk * BLK, BLK)

        def rows_pj(r, carry):
            rows = pl.ds(pl.multiple_of(r * CH, CH), CH)
            part[blk, rows, :] = dot(normed[rows, :], WO[:, pl.ds(off, BLK)]).astype(BF16)
            return carry

        lax.fori_loop(0, NCH, rows_pj, 0)
        sb_msg(o).start()

    def add_rows(blk, start, count, refs):
        def one(r, carry):
            rows = pl.ds(pl.multiple_of(start + r * CH, CH), CH)
            s = part[blk, rows, :].astype(F32)
            for ref in refs:
                s = s + ref[pl.ds(pl.multiple_of(r * CH, CH), CH), :].astype(F32)
            part[blk, rows, :] = s.astype(BF16)
            return carry

        lax.fori_loop(0, count // CH, one, 0)

    def px2(j):
        return rdma(ph(B(1 + 2 * j, 2), c), pxr.at[j], pxs.at[j], pxq.at[j], pn)

    def ydev(d):
        return yp if d == 0 else ym

    def m1(j, d):
        k = d * 2 + j
        return rdma(pq(B(2 * j, 2), d), m1r.at[d, j], m1s.at[k], m1q.at[k], ydev(d))

    def m2(b, d):
        k = d * 4 + b
        blk = B(b, 1 if d == 0 else 3)
        if b % 2 == 1:
            return rdma(ph(blk, c), rd.at[d, b], m2s.at[k], m2q.at[k], ydev(d))
        return rdma(
            pq(blk, 1 - d), rd.at[d, b, pl.ds((1 - d) * QTR, QTR)], m2s.at[k], m2q.at[k], ydev(d)
        )

    def m3(j, d):
        k = d * 2 + j
        blk = B(2 * j, 1 if d == 0 else 3)
        return rdma(
            pq(blk, d), rd.at[d, 2 * j, pl.ds(d * QTR, QTR)], m3s.at[k], m3q.at[k], ydev(d)
        )

    mine_row = c * HALF

    for o in range(4):
        proj(o)
    for o in (0, 1):
        sb_msg(o).wait_recv()
        add_rows(B(*ORDER[o]), mine_row, HALF, (sibr.at[o],))
        px2(o).start()
    for o in range(4, 8):
        proj(o)
    for j in range(2):
        sb_msg(2 + j).wait_recv()
        px2(j).wait_recv()
        add_rows(B(2 * j, 2), mine_row, HALF, (sibr.at[2 + j], pxr.at[j]))
        m1(j, 0).start()
        m1(j, 1).start()
    for o in range(4, 12):
        if o < 8:
            proj(o + 4)
        b, dy = ORDER[o]
        sb_msg(o).wait_recv()
        add_rows(B(b, dy), mine_row, HALF, (sibr.at[o],))
        m2(b, 0 if dy == 1 else 1).start()
    for j in range(2):
        for d in range(2):
            m1(j, d).wait_recv()
            add_rows(B(2 * j, 1 if d == 0 else 3), mine_row + d * QTR, QTR, (m1r.at[d, j],))
            m3(j, d).start()
        proj(12 + 2 * j)
        proj(13 + 2 * j)

    def xb(j):
        return rdma(ph(B(3 - 2 * j, 0), c), xbr.at[j], xbs.at[j], xbq.at[j], pn)

    fin_p = rdma(ph(B(2, 0), c), fin.at[pl.ds(c * HALF, HALF)], fns.at[0], fnr.at[c], at(p, xp))
    fin_s = rdma(ph(own, c), fin.at[pl.ds(c * HALF, HALF)], fns.at[1], fnr.at[2], sib)

    for o in (12, 13, 14, 15):
        b = ORDER[o][0]
        sb_msg(o).wait_recv()
        for d in range(2):
            m2(b, d).wait_recv()
            if b % 2 == 0:
                m3(b // 2, d).wait_recv()
        refs = [sibr.at[o], rd.at[0, b], rd.at[1, b]]
        if b == 2:
            xb(0).wait_recv()
            refs.append(xbr.at[0])
        if b == 0:
            xb(1).wait_recv()
            refs.append(xbr.at[1])
        add_rows(B(b, 0), mine_row, HALF, refs)
        if b == 3:
            xb(0).start()
        if b == 1:
            xb(1).start()
        if b == 2:
            fin_p.start()

    @pl.when(native)
    def _():
        def put(r, carry):
            rows = pl.ds(pl.multiple_of(mine_row + r * CH, CH), CH)
            out_ref[rows, :] = part[own, rows, :]
            return carry

        lax.fori_loop(0, 2, put, 0)
        other_row = (1 - c) * HALF
        rdma(
            ph(own, 1 - c), fin.at[pl.ds(other_row, HALF)], fns.at[1], fnr.at[2], sib
        ).wait_recv()

        def put2(r, carry):
            rows = pl.ds(pl.multiple_of(other_row + r * CH, CH), CH)
            out_ref[rows, :] = fin[rows, :]
            return carry

        lax.fori_loop(0, 2, put2, 0)

    @pl.when(foreign)
    def _():
        fin_s.start()
        for half in range(2):
            dst = fin.at[pl.ds(half * HALF, HALF)]
            rdma(ph(B(2, 0), half), dst, fns.at[0], fnr.at[half], at(p, xp)).wait_recv()

            def put(r, carry):
                rows = pl.ds(pl.multiple_of(half * HALF + r * CH, CH), CH)
                out_ref[rows, :] = fin[rows, :]
                return carry

            lax.fori_loop(0, 2, put, 0)
        fin_s.wait_send()

    esend(0).wait_send()
    esend(1).wait_send()
    e3.wait_send()
    for b in range(4):
        if b % 2 == 0:
            for k in range(6):
                ym_q(b, 0, 0, k, yp).wait_send()
        else:
            ym_h(b, 0, 0, yp).wait_send()
            ym_h(b, 0, 3, ym).wait_send()
        for dy in range(4):
            if (b, dy) != (0, 0):
                sf(b, dy).wait_send()
    for j in range(2):
        pxsend(j).wait_send()
        px2(j).wait_send()
        xb(j).wait_send()
        for d in range(2):
            m1(j, d).wait_send()
            m3(j, d).wait_send()
    for b in range(4):
        for d in range(2):
            m2(b, d).wait_send()
    for o in range(16):
        sb_msg(o).wait_send()
    fin_p.wait_send()
    for buf, sems in ((ctot, tsem), (cst, csem)):
        for k in range(4):
            ring(buf, sems, 0, k, z, zp).wait_send()
        for k in range(3):
            ring(buf, sems, 1, k, z, zm).wait_send()
    tsend.wait_send()
    ssend.wait_send()
    ent_send.wait_send()

    @pl.when(native)
    def _():
        e0.wait_send()
        for m in range(2):
            for d in range(2):
                kv(m, d, z, 0, par).wait_send()
        for k in range(4):
            qmsg(k).wait_send()
        pri_send.wait_send()
        for o in range(16):
            wo_msg(o, o).wait_send()

    @pl.when(foreign)
    def _():
        rate_send.wait_send()
        for k in range(1, 8):
            for m in range(2):
                for d in range(2):
                    kv(m, d, z, k, zp).wait_send()


def local(tokens, w_qkv, w_out, decay_rate, prior_state):
    anyspec = pl.BlockSpec(memory_space=pl.ANY)
    vspec = pl.BlockSpec(memory_space=pltpu.VMEM)
    V = pltpu.VMEM

    def D(n):
        return [pltpu.SemaphoreType.DMA((n,))] * 2

    return pl.pallas_call(
        kernel,
        out_shape=jax.ShapeDtypeStruct((TOK, BLK), BF16),
        in_specs=[anyspec, anyspec, anyspec, vspec, anyspec],
        out_specs=vspec,
        scratch_shapes=[
            V((16, TOK, BLK), BF16),
            V((TOK, BLK), BF16),
            V((3, 4096, BLK), BF16),
            V((BLK, 4096), BF16),
            V((2, DH, DH), F32),
            V((2, TOK), F32),
            V((2, TOK, BLK), F32),
            V((TOK, BLK), F32),
            V((3, TOK, BLK), BF16),
            V((8, CH, CH), F32),
            V((8, CH, DH), F32),
            V((8, CH, DH), F32),
            V((8, 8, DH), F32),
            V((2, 8, DH), F32),
            V((2, 8, DH), F32),
            V((NZ, 2, 8, DH), F32),
            V((8, DH, DH), F32),
            V((2, DH, DH), F32),
            V((2, DH, DH), F32),
            V((NZ, DH, DH), BF16),
            V((2, DH, DH), F32),
            V((8, DH, DH), BF16),
            V((TOK, BLK), BF16),
            V((16, TOK, BLK), BF16),
            V((16, HALF, BLK), BF16),
            V((2, HALF, BLK), BF16),
            V((2, 2, QTR, BLK), BF16),
            V((2, 4, HALF, BLK), BF16),
            V((2, HALF, BLK), BF16),
            V((TOK, BLK), BF16),
            pltpu.SemaphoreType.DMA((6,)),
            *D(4),
            *D(24),
            *D(2),
            *D(16),
            *D(32),
            *D(4),
            *D(16),
            *D(5),
            *D(8),
            *D(8),
            *D(16),
            *D(2),
            *D(4),
            *D(8),
            *D(4),
            *D(2),
            *D(3),
        ],
        compiler_params=pltpu.CompilerParams(
            collective_id=0, has_side_effects=True, vmem_limit_bytes=60 * 1024 * 1024
        ),
    )(tokens, w_qkv, w_out, decay_rate, prior_state)


def solution(mesh):
    in_specs = (
        P("seq", "head"),
        P(None, None, "head"),
        P("head", None),
        P("head", "seq"),
        P("head", None, None),
    )
    out_specs = P("seq", "head")
    return jax.shard_map(local, mesh=mesh, in_specs=in_specs, out_specs=out_specs, check_vma=False)
```

```python
import jax
import jax.numpy as jnp
from jax import lax
from jax.experimental import pallas as pl
from jax.experimental.pallas import tpu as pltpu
from jax.sharding import PartitionSpec as P

F32 = jnp.float32
BF16 = jnp.bfloat16
TOK = 1024
HALF = 512
BLK = 256
CH = 256
NCH = TOK // CH
DH = 128
NZ = 8


def dot(a, b):
    return jnp.dot(a, b, preferred_element_type=F32)


def dot_nt(a, b):
    return lax.dot_general(a, b, (((1,), (1,)), ((), ())), preferred_element_type=F32)


def dot_tn(a, b):
    return lax.dot_general(a, b, (((0,), (0,)), ((), ())), preferred_element_type=F32)


def kernel(
    tok_hbm, wqkv_hbm, wout_hbm, rate_ref, prior_hbm, out_ref,
    X, W, WO, PRI, acc, qkv, dec, sa, sb, ce, tails, tsib, ctot,
    sloc, sown, ssib, cst, est, sful, normed, part,
    rm1, rd, qm1, qd,
    lsem, us, ur, vs, vr, ps, pr, p2s, p2r, ts, tr, cs, cr, ss, sr,
):
    seq = lax.axis_index("seq")
    head = lax.axis_index("head")
    z = seq // 2
    core = seq % 2
    y = head // 4
    x = head % 4
    first = core == 0
    u = jnp.where(first, x, y)
    v = jnp.where(first, y, x)
    su = jnp.where(first, 1, 4)
    sv = jnp.where(first, 4, 1)

    def hid(du, dv):
        return ((u + du) % 4) * su + ((v + dv) % 4) * sv

    own = hid(0, 0)
    up, um = (seq, hid(1, 0)), (seq, hid(3, 0))
    vp, vm = (seq, hid(0, 1)), (seq, hid(0, 3))
    zp = (((z + 1) % NZ) * 2 + core, head)
    zm = (((z + NZ - 1) % NZ) * 2 + core, head)
    sib = (z * 2 + 1 - core, head)

    def rdma(src, dst, s, r, dev):
        return pltpu.make_async_remote_copy(
            src_ref=src, dst_ref=dst, send_sem=s, recv_sem=r,
            device_id=dev, device_id_type=pl.DeviceIdType.MESH,
        )

    ltok = pltpu.make_async_copy(tok_hbm, X.at[own], lsem.at[0])
    lw = pltpu.make_async_copy(wqkv_hbm, W, lsem.at[1])
    lwo = pltpu.make_async_copy(wout_hbm, WO, lsem.at[2])
    lpri = pltpu.make_async_copy(prior_hbm, PRI, lsem.at[3])
    ltok.start()
    lw.start()
    lwo.start()
    lpri.start()

    barrier = pltpu.get_barrier_semaphore()
    for dev in (up, um, vp, vm, zp, zm, sib):
        pl.semaphore_signal(barrier, inc=1, device_id=dev, device_id_type=pl.DeviceIdType.MESH)
    pl.semaphore_wait(barrier, 7)
    ltok.wait()

    def xs(blk, hf):
        return X.at[blk, pl.ds(hf * HALF, HALF)]

    def ag(blk, hf, sems, k, dev):
        return rdma(xs(blk, hf), xs(blk, hf), sems[0].at[k], sems[1].at[k], dev)

    usem, vsem = (us, ur), (vs, vr)
    DU = (0, 3, 1, 2)

    def vsend(b, hf):
        blk = hid(DU[b], 0)
        if hf == 0:
            ag(blk, 0, vsem, 6 * b + 0, vp).start()
            ag(blk, 0, vsem, 6 * b + 4, vm).start()
        else:
            ag(blk, 1, vsem, 6 * b + 3, vm).start()
            ag(blk, 1, vsem, 6 * b + 1, vp).start()

    ag(own, 0, usem, 0, up).start()
    ag(own, 1, usem, 3, um).start()
    ag(own, 1, usem, 1, up).start()
    ag(own, 0, usem, 4, um).start()
    vsend(0, 0)
    vsend(0, 1)

    rowi = lax.broadcasted_iota(jnp.int32, (CH, CH), 0)
    coli = lax.broadcasted_iota(jnp.int32, (CH, CH), 1)
    for h in range(2):
        def one_decay(c, carry):
            i = h * NCH + c
            r = rate_ref[h : h + 1, pl.ds(pl.multiple_of(c * CH, CH), CH)]
            rb = jnp.broadcast_to(r, (CH, CH))
            zero = jnp.zeros((CH, CH), F32)
            c_col = jnp.sum(jnp.where(coli <= rowi, rb, zero), axis=1, keepdims=True)
            r_col = jnp.sum(jnp.where(coli == rowi, rb, zero), axis=1, keepdims=True)
            c_row = jnp.sum(
                jnp.where(rowi <= coli, jnp.broadcast_to(r_col, (CH, CH)), zero),
                axis=0, keepdims=True,
            )
            total = jnp.sum(r, axis=1, keepdims=True)
            gap = jnp.maximum(c_col - c_row, 0.0)
            dec[i] = jnp.where(rowi >= coli, jnp.exp(-gap), zero)
            sa[i] = jnp.broadcast_to(jnp.exp(-c_col), (CH, DH))
            sb[i] = jnp.broadcast_to(jnp.exp(-jnp.maximum(total - c_col, 0.0)), (CH, DH))
            ce[i] = jnp.broadcast_to(total, (8, DH))
            return carry

        lax.fori_loop(0, NCH, one_decay, 0)
        tails[h] = ce[h * NCH] + ce[h * NCH + 1] + ce[h * NCH + 2] + ce[h * NCH + 3]

    tsend = rdma(tails, tsib, ss.at[0], sr.at[0], sib)
    tsend.start()

    def zero_acc(i, carry):
        acc[i // 4, pl.ds((i % 4) * CH, CH)] = jnp.zeros((CH, BLK), F32)
        return carry

    lax.fori_loop(0, 12, zero_acc, 0)

    ag(hid(3, 0), 0, usem, 0, up).wait_recv()
    ag(hid(3, 0), 0, usem, 2, up).start()
    ag(hid(1, 0), 1, usem, 3, um).wait_recv()
    ag(hid(1, 0), 1, usem, 5, um).start()
    vsend(1, 0)
    vsend(2, 1)
    ag(hid(3, 0), 1, usem, 1, up).wait_recv()
    vsend(1, 1)
    ag(hid(1, 0), 0, usem, 4, um).wait_recv()
    vsend(2, 0)
    ag(hid(2, 0), 0, usem, 2, up).wait_recv()
    vsend(3, 0)
    ag(hid(2, 0), 1, usem, 5, um).wait_recv()
    vsend(3, 1)

    lw.wait()

    def mm(blk):
        off = pl.multiple_of(blk * BLK, BLK)

        def rows_mm(r, carry):
            rows = pl.ds(pl.multiple_of(r * CH, CH), CH)
            xt = X[blk, rows, :]
            for c in range(3):
                acc[c, rows, :] += dot(xt, W[c, pl.ds(off, BLK), :])
            return carry

        lax.fori_loop(0, NCH, rows_mm, 0)

    tsend.wait_recv()
    ctot[z] = tails[...] + tsib[...]

    def ring(buf, sems, d, k, slot, dev):
        return rdma(buf.at[slot], buf.at[slot], sems[0].at[d * 4 + k], sems[1].at[d * 4 + k], dev)

    def ring_start(buf, sems):
        ring(buf, sems, 0, 0, z, zp).start()
        ring(buf, sems, 1, 0, z, zm).start()

    def ring_step(buf, sems, k):
        a = (z + NZ - k) % NZ
        ring(buf, sems, 0, k - 1, a, zp).wait_recv()
        if k < 4:
            ring(buf, sems, 0, k, a, zp).start()
            b = (z + k) % NZ
            ring(buf, sems, 1, k - 1, b, zm).wait_recv()
            if k < 3:
                ring(buf, sems, 1, k, b, zm).start()

    tsem, csem = (ts, tr), (cs, cr)
    ring_start(ctot, tsem)

    for b in range(4):
        ag(hid(DU[b], 3), 0, vsem, 6 * b + 0, vp).wait_recv()
        ag(hid(DU[b], 3), 0, vsem, 6 * b + 2, vp).start()
        ag(hid(DU[b], 1), 1, vsem, 6 * b + 3, vm).wait_recv()
        ag(hid(DU[b], 1), 1, vsem, 6 * b + 5, vm).start()
        mm(hid(DU[b], 0))
        ring_step(ctot, tsem, b + 1)

    def du_of(b):
        return jnp.where(b == 1, 3, jnp.where(b == 2, 1, jnp.where(b == 3, 2, 0)))

    def gather_near(b, carry):
        du = du_of(b)
        ag(hid(du, 3), 1, vsem, 6 * b + 1, vp).wait_recv()
        mm(hid(du, 3))
        ag(hid(du, 1), 0, vsem, 6 * b + 4, vm).wait_recv()
        mm(hid(du, 1))
        return carry

    def gather_far(b, carry):
        du = du_of(b)
        ag(hid(du, 2), 0, vsem, 6 * b + 2, vp).wait_recv()
        ag(hid(du, 2), 1, vsem, 6 * b + 5, vm).wait_recv()
        mm(hid(du, 2))
        return carry

    lax.fori_loop(0, 4, gather_near, 0)
    lax.fori_loop(0, 4, gather_far, 0)

    def to_bf16(i, carry):
        rows = pl.ds(pl.multiple_of((i % 4) * CH, CH), CH)
        qkv[i // 4, rows, :] = acc[i // 4, rows, :].astype(BF16)
        return carry

    lax.fori_loop(4, 12, to_bf16, 0)
    def s_msg(hd, k):
        return rdma(sown.at[hd], ssib.at[hd], ss.at[k], sr.at[k], sib)

    for turn, hd in ((1, 1 - core), (3, core)):
        lanes = pl.ds(pl.multiple_of(hd * DH, DH), DH)
        state = jnp.zeros((DH, DH), F32)
        for c in range(NCH):
            i = hd * NCH + c
            rows = pl.ds(c * CH, CH)
            ks = (qkv[1, rows, lanes].astype(F32) * sb[i]).astype(BF16)
            kv = dot_tn(ks, qkv[2, rows, lanes])
            sloc[i] = state
            state = jnp.exp(-ce[i, 0:1, :]) * state + kv
        sown[hd] = state
        s_msg(hd, turn).start()
    lax.fori_loop(0, 4, to_bf16, 0)

    def intra(c):
        rows = slice(c * CH, (c + 1) * CH)
        for h in range(2):
            lanes = slice(h * DH, (h + 1) * DH)
            s = dot_nt(qkv[0, rows, lanes], qkv[1, rows, lanes])
            w = (s * dec[h * NCH + c]).astype(BF16)
            acc[0, rows, lanes] = dot(w, qkv[2, rows, lanes])

    s_msg(core, 1).wait_recv()
    mine, other = sown[core], ssib[core]
    t_own, t_sib = tails[core, 0:1, :], tsib[core, 0:1, :]
    s_even = jnp.where(first, mine, other)
    s_odd = jnp.where(first, other, mine)
    t_odd = jnp.where(first, t_sib, t_own)
    cst[z] = (jnp.exp(-t_odd) * s_even + s_odd).astype(BF16)
    ring_start(cst, csem)
    for k in range(4):
        intra(k)
        ring_step(cst, csem, k + 1)

    lpri.wait()
    run = jnp.zeros((1, DH), F32)
    ent = jnp.zeros((DH, DH), F32)
    for i in range(NZ - 1, -1, -1):
        earlier = i < z
        ent = ent + jnp.where(earlier, jnp.exp(-run) * cst[i].astype(F32), 0.0)
        run = run + jnp.where(earlier, ctot[i, core, 0:1, :], 0.0)
    est[core] = ent + jnp.exp(-run) * PRI[core]
    esend = rdma(est.at[core], est.at[core], ss.at[2], sr.at[2], sib)
    esend.start()
    rdma(est.at[1 - core], est.at[1 - core], ss.at[2], sr.at[2], sib).wait_recv()

    s_msg(1 - core, 3).wait_recv()

    for h in range(2):
        e = est[h]
        e = jnp.where(first, e, jnp.exp(-tsib[h, 0:1, :]) * e + ssib[h])
        before = jnp.zeros((1, DH), F32)
        for c in range(NCH):
            i = h * NCH + c
            sful[i] = (sloc[i] + jnp.exp(-before) * e).astype(BF16)
            before = before + ce[i, 0:1, :]

    def finish_chunk(c):
        rows = slice(c * CH, (c + 1) * CH)
        for h in range(2):
            lanes = slice(h * DH, (h + 1) * DH)
            i = h * NCH + c
            f = dot(qkv[0, rows, lanes], sful[i])
            comb = acc[0, rows, lanes] + f * sa[i]
            ms = jnp.mean(comb * comb, axis=1, keepdims=True)
            normed[rows, lanes] = (comb * lax.rsqrt(ms + 1e-06)).astype(BF16)

    lwo.wait()
    RU = (2, 1, 3, 0)

    def ru_of(i):
        return jnp.where(i == 0, 2, jnp.where(i == 1, 1, jnp.where(i == 2, 3, 0)))

    def proj(blk):
        off = pl.multiple_of(blk * BLK, BLK)

        def rows_pj(r, carry):
            rows = pl.ds(pl.multiple_of(r * CH, CH), CH)
            part[blk, rows, :] = dot(normed[rows, :], WO[:, pl.ds(off, BLK)]).astype(BF16)
            return carry

        lax.fori_loop(0, NCH, rows_pj, 0)

    def ph(blk, hf):
        return part.at[blk, pl.ds(hf * HALF, HALF)]

    def m1(i, d):
        return rdma(
            ph(hid(ru_of(i), 2), d), rm1.at[d, i], ps.at[6 * i + 3 * d], pr.at[6 * i + 3 * d],
            vp if d == 0 else vm,
        )

    def m2(i, d):
        return rdma(
            ph(hid(ru_of(i), 1 if d == 0 else 3), 1 - d), rd.at[d, i, pl.ds((1 - d) * HALF, HALF)],
            ps.at[6 * i + 3 * d + 1], pr.at[6 * i + 3 * d + 1], vp if d == 0 else vm,
        )

    def m3(i, d):
        return rdma(
            ph(hid(ru_of(i), 1 if d == 0 else 3), d), rd.at[d, i, pl.ds(d * HALF, HALF)],
            ps.at[6 * i + 3 * d + 2], pr.at[6 * i + 3 * d + 2], vp if d == 0 else vm,
        )

    def add_half(blk, hf, ref):
        for r in range(2):
            rows = pl.ds(hf * HALF + r * CH, CH)
            part[blk, rows, :] = (
                part[blk, rows, :].astype(F32) + ref[pl.ds(r * CH, CH), :].astype(F32)
            ).astype(BF16)

    def rs1(i):
        proj(hid(RU[i], 2))
        m1(i, 0).start()
        m1(i, 1).start()

    def rs2(i):
        for d in range(2):
            proj(hid(RU[i], 1 if d == 0 else 3))
            m2(i, d).start()

    def rs3(i):
        for d in range(2):
            m1(i, d).wait_recv()
            add_half(hid(RU[i], 1 if d == 0 else 3), d, rm1.at[d, i])
            m3(i, d).start()
        proj(hid(RU[i], 0))

    def q1(d):
        return rdma(ph(hid(2, 0), d), qm1.at[d], p2s.at[3 * d], p2r.at[3 * d], up if d == 0 else um)

    def q2(d):
        return rdma(
            ph(hid(1 if d == 0 else 3, 0), 1 - d), qd.at[d, pl.ds((1 - d) * HALF, HALF)],
            p2s.at[3 * d + 1], p2r.at[3 * d + 1], up if d == 0 else um,
        )

    def q3(d):
        return rdma(
            ph(hid(1 if d == 0 else 3, 0), d), qd.at[d, pl.ds(d * HALF, HALF)],
            p2s.at[3 * d + 2], p2r.at[3 * d + 2], up if d == 0 else um,
        )

    def rs4(i):
        blk = hid(RU[i], 0)
        for d in range(2):
            m2(i, d).wait_recv()
            m3(i, d).wait_recv()

        def reduce_rows(r, carry):
            rows = pl.ds(pl.multiple_of(r * CH, CH), CH)
            part[blk, rows, :] = (
                part[blk, rows, :].astype(F32)
                + rd[0, i, rows, :].astype(F32)
                + rd[1, i, rows, :].astype(F32)
            ).astype(BF16)
            return carry

        lax.fori_loop(0, NCH, reduce_rows, 0)

    def q_add(d):
        q1(d).wait_recv()
        add_half(hid(1 if d == 0 else 3, 0), d, qm1.at[d])
        q3(d).start()

    far = hid(2, 2)
    far_off = pl.multiple_of(far * BLK, BLK)
    for c in range(NCH):
        finish_chunk(c)
        rows = slice(c * CH, (c + 1) * CH)
        part[far, rows, :] = dot(normed[rows, :], WO[:, pl.ds(far_off, BLK)]).astype(BF16)
        if c % 2 == 1:
            m1(0, c // 2).start()
    rs2(0)
    rs1(1)
    rs3(0)
    rs2(1)
    rs1(2)
    rs3(1)
    rs4(0)
    q1(0).start()
    q1(1).start()
    rs2(2)
    rs1(3)
    rs3(2)
    rs4(1)
    q2(0).start()
    rs2(3)
    q_add(0)
    rs3(3)
    rs4(2)
    q2(1).start()
    q_add(1)
    rs4(3)
    for d in range(2):
        q2(d).wait_recv()
    for d in range(2):
        q3(d).wait_recv()

    def finish(r, carry):
        rows = pl.ds(pl.multiple_of(r * CH, CH), CH)
        out_ref[rows, :] = (
            part[own, rows, :].astype(F32) + qd[0, rows, :].astype(F32) + qd[1, rows, :].astype(F32)
        ).astype(BF16)
        return carry

    lax.fori_loop(0, NCH, finish, 0)

    for k in range(6):
        ag(own, 0, usem, k, up).wait_send()

    def drain_ag(k, carry):
        ag(own, 0, vsem, k, vp).wait_send()
        return carry

    lax.fori_loop(0, 24, drain_ag, 0)
    for buf, sems in ((ctot, tsem), (cst, csem)):
        for k in range(4):
            ring(buf, sems, 0, k, z, zp).wait_send()
        for k in range(3):
            ring(buf, sems, 1, k, z, zm).wait_send()
    tsend.wait_send()
    s_msg(1 - core, 1).wait_send()
    s_msg(core, 3).wait_send()
    esend.wait_send()

    def drain_rs(i, carry):
        for d in range(2):
            m1(i, d).wait_send()
            m2(i, d).wait_send()
            m3(i, d).wait_send()
        return carry

    lax.fori_loop(0, 4, drain_rs, 0)
    for d in range(2):
        q1(d).wait_send()
        q2(d).wait_send()
        q3(d).wait_send()


def local(tokens, w_qkv, w_out, decay_rate, prior_state):
    anyspec = pl.BlockSpec(memory_space=pl.ANY)
    vspec = pl.BlockSpec(memory_space=pltpu.VMEM)
    V = pltpu.VMEM
    D = pltpu.SemaphoreType.DMA
    return pl.pallas_call(
        kernel,
        out_shape=jax.ShapeDtypeStruct((TOK, BLK), BF16),
        in_specs=[anyspec, anyspec, anyspec, vspec, anyspec],
        out_specs=vspec,
        scratch_shapes=[
            V((16, TOK, BLK), BF16),
            V((3, 4096, BLK), BF16),
            V((BLK, 4096), BF16),
            V((2, DH, DH), F32),
            V((3, TOK, BLK), F32),
            V((3, TOK, BLK), BF16),
            V((8, CH, CH), F32),
            V((8, CH, DH), F32),
            V((8, CH, DH), F32),
            V((8, 8, DH), F32),
            V((2, 8, DH), F32),
            V((2, 8, DH), F32),
            V((NZ, 2, 8, DH), F32),
            V((8, DH, DH), F32),
            V((2, DH, DH), F32),
            V((2, DH, DH), F32),
            V((NZ, DH, DH), BF16),
            V((2, DH, DH), F32),
            V((8, DH, DH), BF16),
            V((TOK, BLK), BF16),
            V((16, TOK, BLK), BF16),
            V((2, 4, HALF, BLK), BF16),
            V((2, 4, TOK, BLK), BF16),
            V((2, HALF, BLK), BF16),
            V((2, TOK, BLK), BF16),
            D((4,)),
            D((6,)), D((6,)),
            D((24,)), D((24,)),
            D((24,)), D((24,)),
            D((6,)), D((6,)),
            D((8,)), D((8,)),
            D((8,)), D((8,)),
            D((4,)), D((4,)),
        ],
        compiler_params=pltpu.CompilerParams(
            collective_id=0, has_side_effects=True, vmem_limit_bytes=60 * 1024 * 1024
        ),
    )(tokens, w_qkv, w_out, decay_rate, prior_state)


def solution(mesh):
    in_specs = (
        P("seq", "head"),
        P(None, None, "head"),
        P("head", None),
        P("head", "seq"),
        P("head", None, None),
    )
    out_specs = P("seq", "head")
    return jax.shard_map(local, mesh=mesh, in_specs=in_specs, out_specs=out_specs, check_vma=False)
```

```python
import jax
import jax.numpy as jnp
from jax import lax
from jax.experimental import pallas as pl
from jax.experimental.pallas import tpu as pltpu
from jax.sharding import PartitionSpec as P

F32 = jnp.float32
BF16 = jnp.bfloat16
TOK = 1024
HALF = 512
BLK = 256
CH = 256
NCH = TOK // CH
DH = 128
NZ = 8


def dot(a, b):
    return jnp.dot(a, b, preferred_element_type=F32)


def dot_nt(a, b):
    return lax.dot_general(a, b, (((1,), (1,)), ((), ())), preferred_element_type=F32)


def dot_tn(a, b):
    return lax.dot_general(a, b, (((0,), (0,)), ((), ())), preferred_element_type=F32)


def kernel(
    tok_hbm, wqkv_hbm, wout_hbm, rate_ref, prior_hbm, out_ref,
    X, W, WO, PRI, acc, qkv, dec, sa, sb, ce, tails, tsib, ctot,
    sloc, sown, ssib, cst, est, sful, normed, part,
    rm1, rd, qm1, qd,
    lsem, us, ur, vs, vr, ps, pr, p2s, p2r, ts, tr, cs, cr, ss, sr,
):
    seq = lax.axis_index("seq")
    head = lax.axis_index("head")
    z = seq // 2
    core = seq % 2
    y = head // 4
    x = head % 4
    first = core == 0
    u = jnp.where(first, x, y)
    v = jnp.where(first, y, x)
    su = jnp.where(first, 1, 4)
    sv = jnp.where(first, 4, 1)

    def hid(du, dv):
        return ((u + du) % 4) * su + ((v + dv) % 4) * sv

    own = hid(0, 0)
    up, um = (seq, hid(1, 0)), (seq, hid(3, 0))
    vp, vm = (seq, hid(0, 1)), (seq, hid(0, 3))
    zp = (((z + 1) % NZ) * 2 + core, head)
    zm = (((z + NZ - 1) % NZ) * 2 + core, head)
    sib = (z * 2 + 1 - core, head)

    def rdma(src, dst, s, r, dev):
        return pltpu.make_async_remote_copy(
            src_ref=src, dst_ref=dst, send_sem=s, recv_sem=r,
            device_id=dev, device_id_type=pl.DeviceIdType.MESH,
        )

    ltok = pltpu.make_async_copy(tok_hbm, X.at[own], lsem.at[0])
    lw = pltpu.make_async_copy(wqkv_hbm, W, lsem.at[1])
    lwo = pltpu.make_async_copy(wout_hbm, WO, lsem.at[2])
    lpri = pltpu.make_async_copy(prior_hbm, PRI, lsem.at[3])
    ltok.start()
    lw.start()
    lwo.start()
    lpri.start()

    barrier = pltpu.get_barrier_semaphore()
    for dev in (up, um, vp, vm, zp, zm, sib):
        pl.semaphore_signal(barrier, inc=1, device_id=dev, device_id_type=pl.DeviceIdType.MESH)
    pl.semaphore_wait(barrier, 7)
    ltok.wait()

    def xs(blk, hf):
        return X.at[blk, pl.ds(hf * HALF, HALF)]

    def ag(blk, hf, sems, k, dev):
        return rdma(xs(blk, hf), xs(blk, hf), sems[0].at[k], sems[1].at[k], dev)

    usem, vsem = (us, ur), (vs, vr)
    DU = (0, 3, 1, 2)

    def vsend(b, hf):
        blk = hid(DU[b], 0)
        if hf == 0:
            ag(blk, 0, vsem, 6 * b + 0, vp).start()
            ag(blk, 0, vsem, 6 * b + 4, vm).start()
        else:
            ag(blk, 1, vsem, 6 * b + 3, vm).start()
            ag(blk, 1, vsem, 6 * b + 1, vp).start()

    ag(own, 0, usem, 0, up).start()
    ag(own, 1, usem, 3, um).start()
    ag(own, 1, usem, 1, up).start()
    ag(own, 0, usem, 4, um).start()
    vsend(0, 0)
    vsend(0, 1)

    rowi = lax.broadcasted_iota(jnp.int32, (CH, CH), 0)
    coli = lax.broadcasted_iota(jnp.int32, (CH, CH), 1)
    for h in range(2):
        def one_decay(c, carry):
            i = h * NCH + c
            r = rate_ref[h : h + 1, pl.ds(pl.multiple_of(c * CH, CH), CH)]
            rb = jnp.broadcast_to(r, (CH, CH))
            zero = jnp.zeros((CH, CH), F32)
            c_col = jnp.sum(jnp.where(coli <= rowi, rb, zero), axis=1, keepdims=True)
            r_col = jnp.sum(jnp.where(coli == rowi, rb, zero), axis=1, keepdims=True)
            c_row = jnp.sum(
                jnp.where(rowi <= coli, jnp.broadcast_to(r_col, (CH, CH)), zero),
                axis=0, keepdims=True,
            )
            total = jnp.sum(r, axis=1, keepdims=True)
            gap = jnp.maximum(c_col - c_row, 0.0)
            dec[i] = jnp.where(rowi >= coli, jnp.exp(-gap), zero)
            sa[i] = jnp.broadcast_to(jnp.exp(-c_col), (CH, DH))
            sb[i] = jnp.broadcast_to(jnp.exp(-jnp.maximum(total - c_col, 0.0)), (CH, DH))
            ce[i] = jnp.broadcast_to(total, (8, DH))
            return carry

        lax.fori_loop(0, NCH, one_decay, 0)
        tails[h] = ce[h * NCH] + ce[h * NCH + 1] + ce[h * NCH + 2] + ce[h * NCH + 3]

    tsend = rdma(tails, tsib, ss.at[0], sr.at[0], sib)
    tsend.start()

    def zero_acc(i, carry):
        acc[i // 4, pl.ds((i % 4) * CH, CH)] = jnp.zeros((CH, BLK), F32)
        return carry

    lax.fori_loop(0, 12, zero_acc, 0)

    ag(hid(3, 0), 0, usem, 0, up).wait_recv()
    ag(hid(3, 0), 0, usem, 2, up).start()
    ag(hid(1, 0), 1, usem, 3, um).wait_recv()
    ag(hid(1, 0), 1, usem, 5, um).start()
    vsend(1, 0)
    vsend(2, 1)
    ag(hid(3, 0), 1, usem, 1, up).wait_recv()
    vsend(1, 1)
    ag(hid(1, 0), 0, usem, 4, um).wait_recv()
    vsend(2, 0)
    ag(hid(2, 0), 0, usem, 2, up).wait_recv()
    vsend(3, 0)
    ag(hid(2, 0), 1, usem, 5, um).wait_recv()
    vsend(3, 1)

    lw.wait()

    def mm(blk):
        off = pl.multiple_of(blk * BLK, BLK)

        def rows_mm(r, carry):
            rows = pl.ds(pl.multiple_of(r * CH, CH), CH)
            xt = X[blk, rows, :]
            for c in range(3):
                acc[c, rows, :] += dot(xt, W[c, pl.ds(off, BLK), :])
            return carry

        lax.fori_loop(0, NCH, rows_mm, 0)

    tsend.wait_recv()
    ctot[z] = tails[...] + tsib[...]

    def ring(buf, sems, d, k, slot, dev):
        return rdma(buf.at[slot], buf.at[slot], sems[0].at[d * 4 + k], sems[1].at[d * 4 + k], dev)

    def ring_start(buf, sems):
        ring(buf, sems, 0, 0, z, zp).start()
        ring(buf, sems, 1, 0, z, zm).start()

    def ring_step(buf, sems, k):
        a = (z + NZ - k) % NZ
        ring(buf, sems, 0, k - 1, a, zp).wait_recv()
        if k < 4:
            ring(buf, sems, 0, k, a, zp).start()
            b = (z + k) % NZ
            ring(buf, sems, 1, k - 1, b, zm).wait_recv()
            if k < 3:
                ring(buf, sems, 1, k, b, zm).start()

    tsem, csem = (ts, tr), (cs, cr)
    ring_start(ctot, tsem)

    for b in range(4):
        ag(hid(DU[b], 3), 0, vsem, 6 * b + 0, vp).wait_recv()
        ag(hid(DU[b], 3), 0, vsem, 6 * b + 2, vp).start()
        ag(hid(DU[b], 1), 1, vsem, 6 * b + 3, vm).wait_recv()
        ag(hid(DU[b], 1), 1, vsem, 6 * b + 5, vm).start()
        mm(hid(DU[b], 0))
        ring_step(ctot, tsem, b + 1)

    def du_of(b):
        return jnp.where(b == 1, 3, jnp.where(b == 2, 1, jnp.where(b == 3, 2, 0)))

    def gather_near(b, carry):
        du = du_of(b)
        ag(hid(du, 3), 1, vsem, 6 * b + 1, vp).wait_recv()
        mm(hid(du, 3))
        ag(hid(du, 1), 0, vsem, 6 * b + 4, vm).wait_recv()
        mm(hid(du, 1))
        return carry

    def gather_far(b, carry):
        du = du_of(b)
        ag(hid(du, 2), 0, vsem, 6 * b + 2, vp).wait_recv()
        ag(hid(du, 2), 1, vsem, 6 * b + 5, vm).wait_recv()
        mm(hid(du, 2))
        return carry

    lax.fori_loop(0, 4, gather_near, 0)
    lax.fori_loop(0, 4, gather_far, 0)

    def to_bf16(i, carry):
        rows = pl.ds(pl.multiple_of((i % 4) * CH, CH), CH)
        qkv[i // 4, rows, :] = acc[i // 4, rows, :].astype(BF16)
        return carry

    lax.fori_loop(4, 12, to_bf16, 0)
    def s_msg(hd, k):
        return rdma(sown.at[hd], ssib.at[hd], ss.at[k], sr.at[k], sib)

    for turn, hd in ((1, 1 - core), (3, core)):
        lanes = pl.ds(pl.multiple_of(hd * DH, DH), DH)
        state = jnp.zeros((DH, DH), F32)
        for c in range(NCH):
            i = hd * NCH + c
            rows = pl.ds(c * CH, CH)
            ks = (qkv[1, rows, lanes].astype(F32) * sb[i]).astype(BF16)
            kv = dot_tn(ks, qkv[2, rows, lanes])
            sloc[i] = state
            state = jnp.exp(-ce[i, 0:1, :]) * state + kv
        sown[hd] = state
        s_msg(hd, turn).start()
    lax.fori_loop(0, 4, to_bf16, 0)

    def intra(c):
        rows = slice(c * CH, (c + 1) * CH)
        for h in range(2):
            lanes = slice(h * DH, (h + 1) * DH)
            s = dot_nt(qkv[0, rows, lanes], qkv[1, rows, lanes])
            w = (s * dec[h * NCH + c]).astype(BF16)
            acc[0, rows, lanes] = dot(w, qkv[2, rows, lanes])

    s_msg(core, 1).wait_recv()
    mine, other = sown[core], ssib[core]
    t_own, t_sib = tails[core, 0:1, :], tsib[core, 0:1, :]
    s_even = jnp.where(first, mine, other)
    s_odd = jnp.where(first, other, mine)
    t_odd = jnp.where(first, t_sib, t_own)
    cst[z] = (jnp.exp(-t_odd) * s_even + s_odd).astype(BF16)
    def c_msg(d):
        to = (((z + d) % NZ) * 2 + core, head)
        return rdma(cst.at[z], cst.at[z], cs.at[d - 1], cr.at[d - 1], to)

    def c_recv(d):
        a = (z + NZ - d) % NZ
        return rdma(cst.at[a], cst.at[a], cs.at[d - 1], cr.at[d - 1], zp)

    for d in (4, 3, 5, 2, 6, 1, 7):
        c_msg(d).start()
    for k in range(4):
        intra(k)
    for d in range(1, 8):
        c_recv(d).wait_recv()

    lpri.wait()
    run = jnp.zeros((1, DH), F32)
    ent = jnp.zeros((DH, DH), F32)
    for i in range(NZ - 1, -1, -1):
        earlier = i < z
        ent = ent + jnp.where(earlier, jnp.exp(-run) * cst[i].astype(F32), 0.0)
        run = run + jnp.where(earlier, ctot[i, core, 0:1, :], 0.0)
    est[core] = ent + jnp.exp(-run) * PRI[core]
    esend = rdma(est.at[core], est.at[core], ss.at[2], sr.at[2], sib)
    esend.start()
    rdma(est.at[1 - core], est.at[1 - core], ss.at[2], sr.at[2], sib).wait_recv()

    s_msg(1 - core, 3).wait_recv()

    for h in range(2):
        e = est[h]
        e = jnp.where(first, e, jnp.exp(-tsib[h, 0:1, :]) * e + ssib[h])
        before = jnp.zeros((1, DH), F32)
        for c in range(NCH):
            i = h * NCH + c
            sful[i] = (sloc[i] + jnp.exp(-before) * e).astype(BF16)
            before = before + ce[i, 0:1, :]

    def finish_chunk(c):
        rows = slice(c * CH, (c + 1) * CH)
        for h in range(2):
            lanes = slice(h * DH, (h + 1) * DH)
            i = h * NCH + c
            f = dot(qkv[0, rows, lanes], sful[i])
            comb = acc[0, rows, lanes] + f * sa[i]
            ms = jnp.mean(comb * comb, axis=1, keepdims=True)
            normed[rows, lanes] = (comb * lax.rsqrt(ms + 1e-06)).astype(BF16)

    lwo.wait()
    RU = (2, 1, 3, 0)

    def ru_of(i):
        return jnp.where(i == 0, 2, jnp.where(i == 1, 1, jnp.where(i == 2, 3, 0)))

    def proj(blk):
        off = pl.multiple_of(blk * BLK, BLK)

        def rows_pj(r, carry):
            rows = pl.ds(pl.multiple_of(r * CH, CH), CH)
            part[blk, rows, :] = dot(normed[rows, :], WO[:, pl.ds(off, BLK)]).astype(BF16)
            return carry

        lax.fori_loop(0, NCH, rows_pj, 0)

    def ph(blk, hf):
        return part.at[blk, pl.ds(hf * HALF, HALF)]

    def m1(i, d):
        return rdma(
            ph(hid(ru_of(i), 2), d), rm1.at[d, i], ps.at[6 * i + 3 * d], pr.at[6 * i + 3 * d],
            vp if d == 0 else vm,
        )

    def m2(i, d):
        return rdma(
            ph(hid(ru_of(i), 1 if d == 0 else 3), 1 - d), rd.at[d, i, pl.ds((1 - d) * HALF, HALF)],
            ps.at[6 * i + 3 * d + 1], pr.at[6 * i + 3 * d + 1], vp if d == 0 else vm,
        )

    def m3(i, d):
        return rdma(
            ph(hid(ru_of(i), 1 if d == 0 else 3), d), rd.at[d, i, pl.ds(d * HALF, HALF)],
            ps.at[6 * i + 3 * d + 2], pr.at[6 * i + 3 * d + 2], vp if d == 0 else vm,
        )

    def add_half(blk, hf, ref):
        for r in range(2):
            rows = pl.ds(hf * HALF + r * CH, CH)
            part[blk, rows, :] = (
                part[blk, rows, :].astype(F32) + ref[pl.ds(r * CH, CH), :].astype(F32)
            ).astype(BF16)

    def rs1(i):
        proj(hid(RU[i], 2))
        m1(i, 0).start()
        m1(i, 1).start()

    def rs2(i):
        for d in range(2):
            proj(hid(RU[i], 1 if d == 0 else 3))
            m2(i, d).start()

    def rs3(i):
        for d in range(2):
            m1(i, d).wait_recv()
            add_half(hid(RU[i], 1 if d == 0 else 3), d, rm1.at[d, i])
            m3(i, d).start()
        proj(hid(RU[i], 0))

    def q1(d):
        return rdma(ph(hid(2, 0), d), qm1.at[d], p2s.at[3 * d], p2r.at[3 * d], up if d == 0 else um)

    def q2(d):
        return rdma(
            ph(hid(1 if d == 0 else 3, 0), 1 - d), qd.at[d, pl.ds((1 - d) * HALF, HALF)],
            p2s.at[3 * d + 1], p2r.at[3 * d + 1], up if d == 0 else um,
        )

    def q3(d):
        return rdma(
            ph(hid(1 if d == 0 else 3, 0), d), qd.at[d, pl.ds(d * HALF, HALF)],
            p2s.at[3 * d + 2], p2r.at[3 * d + 2], up if d == 0 else um,
        )

    def rs4(i):
        blk = hid(RU[i], 0)
        for d in range(2):
            m2(i, d).wait_recv()
            m3(i, d).wait_recv()

        def reduce_rows(r, carry):
            rows = pl.ds(pl.multiple_of(r * CH, CH), CH)
            part[blk, rows, :] = (
                part[blk, rows, :].astype(F32)
                + rd[0, i, rows, :].astype(F32)
                + rd[1, i, rows, :].astype(F32)
            ).astype(BF16)
            return carry

        lax.fori_loop(0, NCH, reduce_rows, 0)

    def q_add(d):
        q1(d).wait_recv()
        add_half(hid(1 if d == 0 else 3, 0), d, qm1.at[d])
        q3(d).start()

    def drain_early():
        for k in range(6):
            ag(own, 0, usem, k, up).wait_send()

        def drain_ag(k, carry):
            ag(own, 0, vsem, k, vp).wait_send()
            return carry

        lax.fori_loop(0, 24, drain_ag, 0)
        for d in range(1, 8):
            c_msg(d).wait_send()
        for buf, sems in ((ctot, tsem),):
            for k in range(4):
                ring(buf, sems, 0, k, z, zp).wait_send()
            for k in range(3):
                ring(buf, sems, 1, k, z, zm).wait_send()
        tsend.wait_send()
        s_msg(1 - core, 1).wait_send()
        s_msg(core, 3).wait_send()
        esend.wait_send()
        for i in range(4):
            for d in range(2):
                m1(i, d).wait_send()
                m2(i, d).wait_send()
                if i < 3:
                    m3(i, d).wait_send()
        for d in range(2):
            q1(d).wait_send()

    far = hid(2, 2)
    far_off = pl.multiple_of(far * BLK, BLK)
    for c in range(NCH):
        finish_chunk(c)
        rows = slice(c * CH, (c + 1) * CH)
        part[far, rows, :] = dot(normed[rows, :], WO[:, pl.ds(far_off, BLK)]).astype(BF16)
        if c % 2 == 1:
            m1(0, c // 2).start()
    rs2(0)
    rs1(1)
    rs3(0)
    rs2(1)
    rs1(2)
    rs3(1)
    rs4(0)
    q1(0).start()
    q1(1).start()
    rs2(2)
    rs1(3)
    rs3(2)
    rs4(1)
    q2(0).start()
    rs2(3)
    q_add(0)
    rs3(3)
    rs4(2)
    q2(1).start()
    q_add(1)
    drain_early()
    for d in range(2):
        m2(3, d).wait_recv()
        m3(3, d).wait_recv()
    for d in range(2):
        q2(d).wait_recv()
    for d in range(2):
        q3(d).wait_recv()

    def finish(r, carry):
        rows = pl.ds(pl.multiple_of(r * CH, CH), CH)
        out_ref[rows, :] = (
            part[own, rows, :].astype(F32)
            + (rd[0, 3, rows, :].astype(F32) + rd[1, 3, rows, :].astype(F32))
            + (qd[0, rows, :].astype(F32) + qd[1, rows, :].astype(F32))
        ).astype(BF16)
        return carry

    lax.fori_loop(0, NCH, finish, 0)

    for d in range(2):
        m3(3, d).wait_send()
        q2(d).wait_send()
        q3(d).wait_send()


def local(tokens, w_qkv, w_out, decay_rate, prior_state):
    anyspec = pl.BlockSpec(memory_space=pl.ANY)
    vspec = pl.BlockSpec(memory_space=pltpu.VMEM)
    V = pltpu.VMEM
    D = pltpu.SemaphoreType.DMA
    return pl.pallas_call(
        kernel,
        out_shape=jax.ShapeDtypeStruct((TOK, BLK), BF16),
        in_specs=[anyspec, anyspec, anyspec, vspec, anyspec],
        out_specs=vspec,
        scratch_shapes=[
            V((16, TOK, BLK), BF16),
            V((3, 4096, BLK), BF16),
            V((BLK, 4096), BF16),
            V((2, DH, DH), F32),
            V((3, TOK, BLK), F32),
            V((3, TOK, BLK), BF16),
            V((8, CH, CH), F32),
            V((8, CH, DH), F32),
            V((8, CH, DH), F32),
            V((8, 8, DH), F32),
            V((2, 8, DH), F32),
            V((2, 8, DH), F32),
            V((NZ, 2, 8, DH), F32),
            V((8, DH, DH), F32),
            V((2, DH, DH), F32),
            V((2, DH, DH), F32),
            V((NZ, DH, DH), BF16),
            V((2, DH, DH), F32),
            V((8, DH, DH), BF16),
            V((TOK, BLK), BF16),
            V((16, TOK, BLK), BF16),
            V((2, 4, HALF, BLK), BF16),
            V((2, 4, TOK, BLK), BF16),
            V((2, HALF, BLK), BF16),
            V((2, TOK, BLK), BF16),
            D((4,)),
            D((6,)), D((6,)),
            D((24,)), D((24,)),
            D((24,)), D((24,)),
            D((6,)), D((6,)),
            D((8,)), D((8,)),
            D((8,)), D((8,)),
            D((4,)), D((4,)),
        ],
        compiler_params=pltpu.CompilerParams(
            collective_id=0, has_side_effects=True, vmem_limit_bytes=60 * 1024 * 1024
        ),
    )(tokens, w_qkv, w_out, decay_rate, prior_state)


def solution(mesh):
    in_specs = (
        P("seq", "head"),
        P(None, None, "head"),
        P("head", None),
        P("head", "seq"),
        P("head", None, None),
    )
    out_specs = P("seq", "head")
    return jax.shard_map(local, mesh=mesh, in_specs=in_specs, out_specs=out_specs, check_vma=False)
```

```python
import jax
import jax.numpy as jnp
from jax import lax
from jax.experimental import pallas as pl
from jax.experimental.pallas import tpu as pltpu
from jax.sharding import PartitionSpec as P

F32 = jnp.float32
BF16 = jnp.bfloat16
TOK = 1024
HALF = 512
BLK = 256
CH = 256
NCH = TOK // CH
DH = 128
NZ = 8


def dot(a, b):
    return jnp.dot(a, b, preferred_element_type=F32)


def dot_nt(a, b):
    return lax.dot_general(a, b, (((1,), (1,)), ((), ())), preferred_element_type=F32)


def dot_tn(a, b):
    return lax.dot_general(a, b, (((0,), (0,)), ((), ())), preferred_element_type=F32)


def kernel(
    tok_hbm, wqkv_hbm, wout_hbm, rate_ref, prior_hbm, out_ref,
    X, W, WO, PRI, acc, qkv, dec, sa, sb, ce, tails, tsib, ctot,
    sloc, sown, ssib, cst, est, sful, normed, part,
    rm1, rd, qm1, qd,
    lsem, us, ur, vs, vr, ps, pr, p2s, p2r, ts, tr, cs, cr, ss, sr,
):
    seq = lax.axis_index("seq")
    head = lax.axis_index("head")
    z = seq // 2
    core = seq % 2
    y = head // 4
    x = head % 4
    first = core == 0
    u = jnp.where(first, x, y)
    v = jnp.where(first, y, x)
    su = jnp.where(first, 1, 4)
    sv = jnp.where(first, 4, 1)

    def hid(du, dv):
        return ((u + du) % 4) * su + ((v + dv) % 4) * sv

    own = hid(0, 0)
    up, um = (seq, hid(1, 0)), (seq, hid(3, 0))
    vp, vm = (seq, hid(0, 1)), (seq, hid(0, 3))
    zp = (((z + 1) % NZ) * 2 + core, head)
    zm = (((z + NZ - 1) % NZ) * 2 + core, head)
    sib = (z * 2 + 1 - core, head)

    def rdma(src, dst, s, r, dev):
        return pltpu.make_async_remote_copy(
            src_ref=src, dst_ref=dst, send_sem=s, recv_sem=r,
            device_id=dev, device_id_type=pl.DeviceIdType.MESH,
        )

    ltok = pltpu.make_async_copy(tok_hbm, X.at[own], lsem.at[0])
    lw = pltpu.make_async_copy(wqkv_hbm, W, lsem.at[1])
    lwo = pltpu.make_async_copy(wout_hbm, WO, lsem.at[2])
    lpri = pltpu.make_async_copy(prior_hbm, PRI, lsem.at[3])
    ltok.start()
    lw.start()
    lwo.start()
    lpri.start()

    barrier = pltpu.get_barrier_semaphore()
    for dev in (up, um, vp, vm, zp, zm, sib):
        pl.semaphore_signal(barrier, inc=1, device_id=dev, device_id_type=pl.DeviceIdType.MESH)
    pl.semaphore_wait(barrier, 7)
    ltok.wait()

    def xs(blk, hf):
        return X.at[blk, pl.ds(hf * HALF, HALF)]

    def ag(blk, hf, sems, k, dev):
        return rdma(xs(blk, hf), xs(blk, hf), sems[0].at[k], sems[1].at[k], dev)

    usem, vsem = (us, ur), (vs, vr)
    DU = (0, 3, 1, 2)

    def vsend(b, hf):
        blk = hid(DU[b], 0)
        if hf == 0:
            ag(blk, 0, vsem, 6 * b + 0, vp).start()
            ag(blk, 0, vsem, 6 * b + 4, vm).start()
        else:
            ag(blk, 1, vsem, 6 * b + 3, vm).start()
            ag(blk, 1, vsem, 6 * b + 1, vp).start()

    ag(own, 0, usem, 0, up).start()
    ag(own, 1, usem, 3, um).start()
    ag(own, 1, usem, 1, up).start()
    ag(own, 0, usem, 4, um).start()
    vsend(0, 0)
    vsend(0, 1)

    rowi = lax.broadcasted_iota(jnp.int32, (CH, CH), 0)
    coli = lax.broadcasted_iota(jnp.int32, (CH, CH), 1)
    for h in range(2):
        def one_decay(c, carry):
            i = h * NCH + c
            r = rate_ref[h : h + 1, pl.ds(pl.multiple_of(c * CH, CH), CH)]
            rb = jnp.broadcast_to(r, (CH, CH))
            zero = jnp.zeros((CH, CH), F32)
            c_col = jnp.sum(jnp.where(coli <= rowi, rb, zero), axis=1, keepdims=True)
            r_col = jnp.sum(jnp.where(coli == rowi, rb, zero), axis=1, keepdims=True)
            c_row = jnp.sum(
                jnp.where(rowi <= coli, jnp.broadcast_to(r_col, (CH, CH)), zero),
                axis=0, keepdims=True,
            )
            total = jnp.sum(r, axis=1, keepdims=True)
            gap = jnp.maximum(c_col - c_row, 0.0)
            dec[i] = jnp.where(rowi >= coli, jnp.exp(-gap), zero)
            sa[i] = jnp.broadcast_to(jnp.exp(-c_col), (CH, DH))
            sb[i] = jnp.broadcast_to(jnp.exp(-jnp.maximum(total - c_col, 0.0)), (CH, DH))
            ce[i] = jnp.broadcast_to(total, (8, DH))
            return carry

        lax.fori_loop(0, NCH, one_decay, 0)
        tails[h] = ce[h * NCH] + ce[h * NCH + 1] + ce[h * NCH + 2] + ce[h * NCH + 3]

    tsend = rdma(tails, tsib, ss.at[0], sr.at[0], sib)
    tsend.start()

    def zero_acc(i, carry):
        acc[i // 4, pl.ds((i % 4) * CH, CH)] = jnp.zeros((CH, BLK), F32)
        return carry

    lax.fori_loop(0, 12, zero_acc, 0)

    ag(hid(3, 0), 0, usem, 0, up).wait_recv()
    ag(hid(3, 0), 0, usem, 2, up).start()
    ag(hid(1, 0), 1, usem, 3, um).wait_recv()
    ag(hid(1, 0), 1, usem, 5, um).start()
    vsend(1, 0)
    vsend(2, 1)
    ag(hid(3, 0), 1, usem, 1, up).wait_recv()
    vsend(1, 1)
    ag(hid(1, 0), 0, usem, 4, um).wait_recv()
    vsend(2, 0)
    ag(hid(2, 0), 0, usem, 2, up).wait_recv()
    vsend(3, 0)
    ag(hid(2, 0), 1, usem, 5, um).wait_recv()
    vsend(3, 1)

    lw.wait()

    def mm(blk):
        off = pl.multiple_of(blk * BLK, BLK)

        def rows_mm(r, carry):
            rows = pl.ds(pl.multiple_of(r * CH, CH), CH)
            xt = X[blk, rows, :]
            for c in range(3):
                acc[c, rows, :] += dot(xt, W[c, pl.ds(off, BLK), :])
            return carry

        lax.fori_loop(0, NCH, rows_mm, 0)

    tsend.wait_recv()
    ctot[z] = tails[...] + tsib[...]

    def ring(buf, sems, d, k, slot, dev):
        return rdma(buf.at[slot], buf.at[slot], sems[0].at[d * 4 + k], sems[1].at[d * 4 + k], dev)

    def ring_start(buf, sems):
        ring(buf, sems, 0, 0, z, zp).start()
        ring(buf, sems, 1, 0, z, zm).start()

    def ring_step(buf, sems, k):
        a = (z + NZ - k) % NZ
        ring(buf, sems, 0, k - 1, a, zp).wait_recv()
        if k < 4:
            ring(buf, sems, 0, k, a, zp).start()
            b = (z + k) % NZ
            ring(buf, sems, 1, k - 1, b, zm).wait_recv()
            if k < 3:
                ring(buf, sems, 1, k, b, zm).start()

    tsem, csem = (ts, tr), (cs, cr)
    ring_start(ctot, tsem)

    for b in range(4):
        ag(hid(DU[b], 3), 0, vsem, 6 * b + 0, vp).wait_recv()
        ag(hid(DU[b], 3), 0, vsem, 6 * b + 2, vp).start()
        ag(hid(DU[b], 1), 1, vsem, 6 * b + 3, vm).wait_recv()
        ag(hid(DU[b], 1), 1, vsem, 6 * b + 5, vm).start()
        mm(hid(DU[b], 0))
        ring_step(ctot, tsem, b + 1)

    def du_of(b):
        return jnp.where(b == 1, 3, jnp.where(b == 2, 1, jnp.where(b == 3, 2, 0)))

    def gather_near(b, carry):
        du = du_of(b)
        ag(hid(du, 3), 1, vsem, 6 * b + 1, vp).wait_recv()
        mm(hid(du, 3))
        ag(hid(du, 1), 0, vsem, 6 * b + 4, vm).wait_recv()
        mm(hid(du, 1))
        return carry

    def gather_far(b, carry):
        du = du_of(b)
        ag(hid(du, 2), 0, vsem, 6 * b + 2, vp).wait_recv()
        ag(hid(du, 2), 1, vsem, 6 * b + 5, vm).wait_recv()
        mm(hid(du, 2))
        return carry

    lax.fori_loop(0, 4, gather_near, 0)
    lax.fori_loop(0, 4, gather_far, 0)

    def to_bf16(i, carry):
        rows = pl.ds(pl.multiple_of((i % 4) * CH, CH), CH)
        qkv[i // 4, rows, :] = acc[i // 4, rows, :].astype(BF16)
        return carry

    lax.fori_loop(4, 12, to_bf16, 0)
    def s_msg(hd, k):
        return rdma(sown.at[hd], ssib.at[hd], ss.at[k], sr.at[k], sib)

    for turn, hd in ((1, 1 - core), (3, core)):
        lanes = pl.ds(pl.multiple_of(hd * DH, DH), DH)
        state = jnp.zeros((DH, DH), F32)
        for c in range(NCH):
            i = hd * NCH + c
            rows = pl.ds(c * CH, CH)
            ks = (qkv[1, rows, lanes].astype(F32) * sb[i]).astype(BF16)
            kv = dot_tn(ks, qkv[2, rows, lanes])
            sloc[i] = state
            state = jnp.exp(-ce[i, 0:1, :]) * state + kv
        sown[hd] = state
        s_msg(hd, turn).start()
    lax.fori_loop(0, 4, to_bf16, 0)

    def intra(c):
        rows = slice(c * CH, (c + 1) * CH)
        for h in range(2):
            lanes = slice(h * DH, (h + 1) * DH)
            s = dot_nt(qkv[0, rows, lanes], qkv[1, rows, lanes])
            w = (s * dec[h * NCH + c]).astype(BF16)
            acc[0, rows, lanes] = dot(w, qkv[2, rows, lanes])

    s_msg(core, 1).wait_recv()
    mine, other = sown[core], ssib[core]
    t_own, t_sib = tails[core, 0:1, :], tsib[core, 0:1, :]
    s_even = jnp.where(first, mine, other)
    s_odd = jnp.where(first, other, mine)
    t_odd = jnp.where(first, t_sib, t_own)
    cst[z] = (jnp.exp(-t_odd) * s_even + s_odd).astype(BF16)
    def c_msg(d):
        to = (((z + d) % NZ) * 2 + core, head)
        return rdma(cst.at[z], cst.at[z], cs.at[d - 1], cr.at[d - 1], to)

    def c_recv(d):
        a = (z + NZ - d) % NZ
        return rdma(cst.at[a], cst.at[a], cs.at[d - 1], cr.at[d - 1], zp)

    for d in (4, 3, 5, 2, 6, 1, 7):
        c_msg(d).start()
    for k in range(4):
        intra(k)
    for d in range(1, 8):
        c_recv(d).wait_recv()

    lpri.wait()
    run = jnp.zeros((1, DH), F32)
    ent = jnp.zeros((DH, DH), F32)
    for i in range(NZ - 1, -1, -1):
        earlier = i < z
        ent = ent + jnp.where(earlier, jnp.exp(-run) * cst[i].astype(F32), 0.0)
        run = run + jnp.where(earlier, ctot[i, core, 0:1, :], 0.0)
    est[core] = ent + jnp.exp(-run) * PRI[core]
    esend = rdma(est.at[core], est.at[core], ss.at[2], sr.at[2], sib)
    esend.start()
    rdma(est.at[1 - core], est.at[1 - core], ss.at[2], sr.at[2], sib).wait_recv()

    s_msg(1 - core, 3).wait_recv()

    for h in range(2):
        e = est[h]
        e = jnp.where(first, e, jnp.exp(-tsib[h, 0:1, :]) * e + ssib[h])
        before = jnp.zeros((1, DH), F32)
        for c in range(NCH):
            i = h * NCH + c
            sful[i] = (sloc[i] + jnp.exp(-before) * e).astype(BF16)
            before = before + ce[i, 0:1, :]

    def finish_chunk(c):
        rows = slice(c * CH, (c + 1) * CH)
        for h in range(2):
            lanes = slice(h * DH, (h + 1) * DH)
            i = h * NCH + c
            f = dot(qkv[0, rows, lanes], sful[i])
            comb = acc[0, rows, lanes] + f * sa[i]
            ms = jnp.mean(comb * comb, axis=1, keepdims=True)
            normed[rows, lanes] = (comb * lax.rsqrt(ms + 1e-06)).astype(BF16)

    lwo.wait()
    RU = (2, 1, 3, 0)

    def ru_of(i):
        return jnp.where(i == 0, 2, jnp.where(i == 1, 1, jnp.where(i == 2, 3, 0)))

    def proj(blk):
        off = pl.multiple_of(blk * BLK, BLK)

        def rows_pj(r, carry):
            rows = pl.ds(pl.multiple_of(r * CH, CH), CH)
            part[blk, rows, :] = dot(normed[rows, :], WO[:, pl.ds(off, BLK)]).astype(BF16)
            return carry

        lax.fori_loop(0, NCH, rows_pj, 0)

    def ph(blk, hf):
        return part.at[blk, pl.ds(hf * HALF, HALF)]

    def m1(i, d):
        return rdma(
            ph(hid(ru_of(i), 2), d), rm1.at[d, i], ps.at[6 * i + 3 * d], pr.at[6 * i + 3 * d],
            vp if d == 0 else vm,
        )

    def m2(i, d):
        return rdma(
            ph(hid(ru_of(i), 1 if d == 0 else 3), 1 - d), rd.at[d, i, pl.ds((1 - d) * HALF, HALF)],
            ps.at[6 * i + 3 * d + 1], pr.at[6 * i + 3 * d + 1], vp if d == 0 else vm,
        )

    def m3(i, d):
        return rdma(
            ph(hid(ru_of(i), 1 if d == 0 else 3), d), rd.at[d, i, pl.ds(d * HALF, HALF)],
            ps.at[6 * i + 3 * d + 2], pr.at[6 * i + 3 * d + 2], vp if d == 0 else vm,
        )

    def add_half(blk, hf, ref):
        for r in range(2):
            rows = pl.ds(hf * HALF + r * CH, CH)
            part[blk, rows, :] = (
                part[blk, rows, :].astype(F32) + ref[pl.ds(r * CH, CH), :].astype(F32)
            ).astype(BF16)

    def rs1(i):
        proj(hid(RU[i], 2))
        m1(i, 0).start()
        m1(i, 1).start()

    def rs2(i):
        for d in range(2):
            proj(hid(RU[i], 1 if d == 0 else 3))
            m2(i, d).start()

    def rs3(i):
        for d in range(2):
            m1(i, d).wait_recv()
            add_half(hid(RU[i], 1 if d == 0 else 3), d, rm1.at[d, i])
            m3(i, d).start()
        proj(hid(RU[i], 0))

    def q1(d):
        return rdma(ph(hid(2, 0), d), qm1.at[d], p2s.at[3 * d], p2r.at[3 * d], up if d == 0 else um)

    def q2(d):
        return rdma(
            ph(hid(1 if d == 0 else 3, 0), 1 - d), qd.at[d, pl.ds((1 - d) * HALF, HALF)],
            p2s.at[3 * d + 1], p2r.at[3 * d + 1], up if d == 0 else um,
        )

    def q3(d):
        return rdma(
            ph(hid(1 if d == 0 else 3, 0), d), qd.at[d, pl.ds(d * HALF, HALF)],
            p2s.at[3 * d + 2], p2r.at[3 * d + 2], up if d == 0 else um,
        )

    def rs4(i):
        blk = hid(RU[i], 0)
        for d in range(2):
            m2(i, d).wait_recv()
            m3(i, d).wait_recv()

        def reduce_rows(r, carry):
            rows = pl.ds(pl.multiple_of(r * CH, CH), CH)
            part[blk, rows, :] = (
                part[blk, rows, :].astype(F32)
                + rd[0, i, rows, :].astype(F32)
                + rd[1, i, rows, :].astype(F32)
            ).astype(BF16)
            return carry

        lax.fori_loop(0, NCH, reduce_rows, 0)

    def q_add(d):
        q1(d).wait_recv()
        add_half(hid(1 if d == 0 else 3, 0), d, qm1.at[d])
        q3(d).start()

    def drain_early():
        for k in range(6):
            ag(own, 0, usem, k, up).wait_send()

        def drain_ag(k, carry):
            ag(own, 0, vsem, k, vp).wait_send()
            return carry

        lax.fori_loop(0, 24, drain_ag, 0)
        for d in range(1, 8):
            c_msg(d).wait_send()
        for buf, sems in ((ctot, tsem),):
            for k in range(4):
                ring(buf, sems, 0, k, z, zp).wait_send()
            for k in range(3):
                ring(buf, sems, 1, k, z, zm).wait_send()
        tsend.wait_send()
        s_msg(1 - core, 1).wait_send()
        s_msg(core, 3).wait_send()
        esend.wait_send()
        for i in range(4):
            for d in range(2):
                m1(i, d).wait_send()
                m2(i, d).wait_send()
                if i < 3:
                    m3(i, d).wait_send()
        for d in range(2):
            q1(d).wait_send()

    far = hid(2, 2)
    far_off = pl.multiple_of(far * BLK, BLK)
    for c in range(NCH):
        finish_chunk(c)
        rows = slice(c * CH, (c + 1) * CH)
        part[far, rows, :] = dot(normed[rows, :], WO[:, pl.ds(far_off, BLK)]).astype(BF16)
        if c % 2 == 1:
            m1(0, c // 2).start()
    rs2(0)
    rs1(1)
    rs3(0)
    rs2(1)
    rs1(2)
    rs3(1)
    rs4(0)
    q1(0).start()
    q1(1).start()
    rs2(2)
    rs1(3)
    rs3(2)
    rs4(1)
    q2(0).start()
    rs2(3)
    q_add(0)
    rs3(3)
    rs4(2)
    q2(1).start()
    q_add(1)
    drain_early()
    for d in range(2):
        m2(3, d).wait_recv()
        m3(3, d).wait_recv()
    for d in range(2):
        q2(d).wait_recv()
    for d in range(2):
        q3(d).wait_recv()

    def finish(r, carry):
        rows = pl.ds(pl.multiple_of(r * CH, CH), CH)
        out_ref[rows, :] = (
            part[own, rows, :].astype(F32)
            + (rd[0, 3, rows, :].astype(F32) + rd[1, 3, rows, :].astype(F32))
            + (qd[0, rows, :].astype(F32) + qd[1, rows, :].astype(F32))
        ).astype(BF16)
        return carry

    lax.fori_loop(0, NCH, finish, 0)

    for d in range(2):
        m3(3, d).wait_send()
        q2(d).wait_send()
        q3(d).wait_send()


def local(tokens, w_qkv, w_out, decay_rate, prior_state):
    anyspec = pl.BlockSpec(memory_space=pl.ANY)
    vspec = pl.BlockSpec(memory_space=pltpu.VMEM)
    V = pltpu.VMEM
    D = pltpu.SemaphoreType.DMA
    return pl.pallas_call(
        kernel,
        out_shape=pltpu.VMEM((TOK, BLK), BF16),
        in_specs=[anyspec, anyspec, anyspec, vspec, anyspec],
        out_specs=vspec,
        scratch_shapes=[
            V((16, TOK, BLK), BF16),
            V((3, 4096, BLK), BF16),
            V((BLK, 4096), BF16),
            V((2, DH, DH), F32),
            V((3, TOK, BLK), F32),
            V((3, TOK, BLK), BF16),
            V((8, CH, CH), F32),
            V((8, CH, DH), F32),
            V((8, CH, DH), F32),
            V((8, 8, DH), F32),
            V((2, 8, DH), F32),
            V((2, 8, DH), F32),
            V((NZ, 2, 8, DH), F32),
            V((8, DH, DH), F32),
            V((2, DH, DH), F32),
            V((2, DH, DH), F32),
            V((NZ, DH, DH), BF16),
            V((2, DH, DH), F32),
            V((8, DH, DH), BF16),
            V((TOK, BLK), BF16),
            V((16, TOK, BLK), BF16),
            V((2, 4, HALF, BLK), BF16),
            V((2, 4, TOK, BLK), BF16),
            V((2, HALF, BLK), BF16),
            V((2, TOK, BLK), BF16),
            D((4,)),
            D((6,)), D((6,)),
            D((24,)), D((24,)),
            D((24,)), D((24,)),
            D((6,)), D((6,)),
            D((8,)), D((8,)),
            D((8,)), D((8,)),
            D((4,)), D((4,)),
        ],
        compiler_params=pltpu.CompilerParams(
            collective_id=0, has_side_effects=True, vmem_limit_bytes=60 * 1024 * 1024
        ),
    )(tokens, w_qkv, w_out, decay_rate, prior_state)


def solution(mesh):
    in_specs = (
        P("seq", "head"),
        P(None, None, "head"),
        P("head", None),
        P("head", "seq"),
        P("head", None, None),
    )
    out_specs = P("seq", "head")
    return jax.shard_map(local, mesh=mesh, in_specs=in_specs, out_specs=out_specs, check_vma=False)
```
